128 devices in a mesh: row: 8 (over x_lo, z), col: 16 (over y, x_hi, core).
Axes of the slice: x: 4 (x_hi: 2, x_lo: 2; x = x_hi * 2 + x_lo), y: 4, z: 4, core: 2. Of those that a mesh axis runs over, the one named last changes fastest.
Arguments:
- amplitudes: bfloat16 [32, 32, 12, 4096], P('row', 'col'), may hold values from -6 to 6
- integrals: bfloat16 [32, 32, 47, 4096], P('row', 'col'), may hold values from -0.125 to 0.125
- pair_lists: int32 [8, 12, 2], replicated, may hold values from 0 to 46, as said below
- tile_counts: int32 [8], replicated, may hold values from 1 to 12, as said below
Outputs:
- symmetric: float32 [32, 32, 12, 4096], P('row', 'col')
The draws below stay inside these ranges and needn't reach their ends.
Inputs may be any that keep to these rules, and one draw needn't show every extreme that they name: `pair_lists`: each grid row lists 12 distinct ordered pairs of different tiles. `tile_counts`: the largest count equals 12.
All inputs are finite; a program needn't handle non-finite values.
Results may differ from the reference program's by a relative error of at most 0.0029.
Values may be sent and summed in bfloat16 or wider, within the bound.
A program may use at most 128 MiB of HBM per device.

```python
import jax
import jax.numpy as jnp
import numpy as np
from jax import lax

TILE = 64
NVT = 47
NP = 12
NOCC = 32
N_ROW = 8


def make_lists(key):
    upper_rows, upper_cols = np.triu_indices(NVT, 1)
    pair_table = jnp.asarray(np.stack([upper_rows, upper_cols], 1).astype(np.int32))
    table_size = pair_table.shape[0]
    forced_index = NVT - 2
    shuffled = jax.random.permutation(jax.random.fold_in(key, 11), table_size).astype(jnp.int32)
    ranking = jnp.where(jnp.arange(table_size, dtype=jnp.int32) == forced_index, -1, shuffled)
    chosen = jnp.argsort(ranking, stable=True)[:NP]
    base_pairs = pair_table[chosen]
    flips = jax.random.randint(jax.random.fold_in(key, 12), (N_ROW, NP, 1), 0, 2)
    oriented = jnp.where(flips == 1, base_pairs[None, :, ::-1], base_pairs[None, :, :])
    row_keys = jax.random.split(jax.random.fold_in(key, 15), N_ROW)
    orders = jax.vmap(lambda row_key: jax.random.permutation(row_key, NP))(row_keys)
    lists = jnp.take_along_axis(oriented, orders[:, :, None], axis=1).astype(jnp.int32)
    counts = jax.random.randint(jax.random.fold_in(key, 13), (N_ROW,), 1, NP + 1)
    full_row = jax.random.randint(jax.random.fold_in(key, 14), (), 0, N_ROW)
    counts = counts.at[full_row].set(NP).astype(jnp.int32)
    return (lists, counts)


def draw_pair_lists(key, part):
    return make_lists(key)[0]


def draw_tile_counts(key, part):
    return make_lists(key)[1]


def block_levels(rng, dims, pieces, low, high):
    def one(axis_at, shards_of):
        draws = jax.random.uniform(jax.random.fold_in(jax.random.fold_in(rng, 6), axis_at), (shards_of,), jnp.float32, low / len(pieces), high / len(pieces))
        return jnp.repeat(jnp.exp(draws), dims[axis_at] // shards_of).reshape((-1,) + (1,) * (len(dims) - axis_at - 1))

    level = one(*pieces[0])
    for cut in pieces[1:]:
        level = level * one(*cut)
    return level


def scatter_about(rng, dims, spread, limit, cuts=(), kind=jnp.bfloat16):
    result = jax.random.normal(rng, dims, jnp.float32) * spread
    if len(cuts) > 0:
        result = block_levels(rng, dims, cuts, -0.22, 0.18) * result
    return jnp.clip(result, min=-limit, max=limit).astype(kind)


def setup_inputs(seed: int = 0) -> dict:
    key_of = jax.random.split(jax.random.key(seed), 5)
    return {
        "amplitudes": scatter_about(key_of[0], (NOCC, NOCC, NP, TILE * TILE), 1.0, 6.0, ((0, 8), (1, 16))),
        "integrals": scatter_about(key_of[1], (NOCC, NOCC, NVT, TILE * TILE), (NOCC * TILE) ** -0.5, 0.125, ((0, 8), (1, 16))),
        "pair_lists": draw_pair_lists(jax.random.fold_in(key_of[4], 71), 0),
        "tile_counts": draw_tile_counts(jax.random.fold_in(key_of[4], 71), 0),
    }


def reference(amplitudes, integrals, pair_lists, tile_counts):
    occ_total = amplitudes.shape[0]
    occ_row = occ_total // N_ROW
    slot_count = amplitudes.shape[2]
    tile_width = TILE
    live_slots = (jnp.arange(slot_count, dtype=jnp.int32)[None, :] < tile_counts[:, None]).astype(jnp.float32)

    def one_row(orbital):
        grid_group = (orbital // occ_row).astype(jnp.int32)
        tiles_b = lax.dynamic_index_in_dim(pair_lists, grid_group, 0, keepdims=False)[:, 1]
        chosen = jnp.take(integrals, tiles_b, axis=2).astype(jnp.float32)
        chosen = chosen.reshape(occ_total, occ_total, slot_count, tile_width, tile_width)
        amp_row = lax.dynamic_index_in_dim(amplitudes, orbital, 0, keepdims=False).astype(jnp.float32)
        amp_row = amp_row.reshape(occ_total, slot_count, tile_width, tile_width)
        row_out = jnp.einsum('ksac,kjscb->jsab', amp_row, chosen)
        keep_slots = lax.dynamic_index_in_dim(live_slots, grid_group, 0, keepdims=False)
        row_out = row_out * keep_slots[None, :, None, None]
        return row_out.reshape(occ_total, slot_count, tile_width * tile_width).astype(jnp.bfloat16)

    cycle = lax.map(one_row, jnp.arange(occ_total, dtype=jnp.int32))
    groups = jnp.arange(occ_total, dtype=jnp.int32) // occ_row
    tile_first = pair_lists[:, :, 0]
    tile_second = pair_lists[:, :, 1]
    pair_match = ((tile_first[:, None, :, None] == tile_second[None, :, None, :])
                  & (tile_second[:, None, :, None] == tile_first[None, :, None, :])).astype(jnp.float32)
    pair_match = pair_match[groups][:, groups]
    mirrored = jnp.swapaxes(cycle, 0, 1).astype(jnp.float32)
    mirrored = mirrored.reshape(occ_total, occ_total, slot_count, tile_width, tile_width)
    crossed = jnp.einsum('ijst,ijtba->ijsab', pair_match, mirrored)
    own_part = cycle.astype(jnp.float32).reshape(occ_total, occ_total, slot_count, tile_width, tile_width)
    keep_all = live_slots[groups]
    symmetric = (own_part + crossed) * keep_all[:, None, :, None, None]
    return symmetric.reshape(occ_total, occ_total, slot_count, tile_width * tile_width)
```

```python
import functools

import jax
import jax.numpy as jnp
import numpy as np
from jax import lax
from jax.experimental import pallas as pl
from jax.experimental.pallas import tpu as pltpu
from jax.sharding import PartitionSpec as P

MESH = pl.DeviceIdType.MESH
ROWS = 8
TILE = 64
HALF = TILE // 2
LANES = 128


def merge_matrix(permute):
    out = np.zeros((2 * LANES, 2 * LANES), np.float32)
    for operand in range(2):
        for h in range(2):
            for c in range(TILE):
                place = (c % 2) * HALF + c // 2 if permute else c
                out[operand * LANES + h * TILE + c, h * LANES + operand * TILE + place] = 1.0
    return out


def untangle_matrix():
    out = np.zeros((LANES, LANES), np.float32)
    for j in range(2):
        for h in range(2):
            for p in range(HALF):
                out[j * TILE + h * HALF + p, j * TILE + 2 * p + h] = 1.0
    return out


def pack_left(amp_ref, mat_ref, out_ref):
    occ, _, slots = amp_ref.shape[:3]
    half = slots // 2
    for i in range(occ):
        left = amp_ref[i, 0].reshape(slots * HALF, LANES)
        right = amp_ref[i, 1].reshape(slots * HALF, LANES)
        both = jnp.concatenate([left, right], axis=1)
        made = jnp.dot(both, mat_ref[...], preferred_element_type=jnp.float32).astype(jnp.bfloat16)
        for h in range(2):
            rows = made[:, h * LANES : (h + 1) * LANES].reshape(2, half, HALF, LANES)
            out_ref[:, :, i * TILE + h * HALF : i * TILE + (h + 1) * HALF, :] = rows


def pack_right(list_ref, int_ref, mat_ref, out_ref):
    row = pl.program_id(0)
    occ = int_ref.shape[0]
    half = out_ref.shape[2]
    for s in range(2 * half):
        tile = list_ref[row, s]
        left = int_ref[:, 0, tile].reshape(occ * HALF, LANES)
        right = int_ref[:, 1, tile].reshape(occ * HALF, LANES)
        both = jnp.concatenate([left, right], axis=1)
        made = jnp.dot(both, mat_ref[...], preferred_element_type=jnp.float32).astype(jnp.bfloat16)
        for k in range(occ):
            for g in range(2):
                out_ref[0, s // half, s % half, k * TILE + g * HALF : k * TILE + (g + 1) * HALF, :] = made[
                    k * HALF : (k + 1) * HALF, g * LANES : (g + 1) * LANES
                ]


def exchange(a_ref, w_ref, own_ref, mir_ref, abuf, wbuf, cbuf, a_send, a_recv, f_send, w_send, w_recv, c_send, c_recv, l_sem):
    row = lax.axis_index("row")
    col = lax.axis_index("col")
    core = lax.rem(col, 2)
    other = 1 - core
    chip = col // 2
    xh = lax.rem(chip, 2)
    y = chip // 2
    xl, z = row // 4, lax.rem(row, 4)
    half = abuf.shape[1]
    diagonal = chip == row

    def col_of(y_at, xh_at, core_at):
        return (lax.rem(y_at, 4) * 2 + xh_at) * 2 + core_at

    def row_of(step):
        return lax.rem(xl + step // 4, 2) * 4 + lax.rem(z + step % 4, 4)

    barrier = pltpu.get_barrier_semaphore()

    def greet(row_at, col_at):
        pl.semaphore_signal(barrier, inc=1, device_id={"row": row_at, "col": col_at}, device_id_type=MESH)

    greet(row, chip * 2 + other)
    for step in range(1, ROWS):
        for e in range(2):
            greet(row_of(step), chip * 2 + e)
    for e in range(2):
        greet(row, col_of(y, 1 - xh, e))
        for dy in range(1, 4):
            greet(row, col_of(y + dy, xh, e))

    @pl.when(jnp.logical_not(diagonal))
    def _():
        for e in range(2):
            greet(chip, row * 2 + e)

    pl.semaphore_wait(barrier, jnp.where(diagonal, 23, 25))

    def remote(src, dst, send, recv, row_at, col_at):
        return pltpu.make_async_remote_copy(
            src_ref=src, dst_ref=dst, send_sem=send, recv_sem=recv,
            device_id={"row": row_at, "col": col_at}, device_id_type=MESH,
        )

    started = []

    def go(copy):
        copy.start()
        started.append(copy)

    for e in range(2):
        go(remote(a_ref.at[e], abuf.at[col], a_send.at[0, e], a_recv.at[col], row, col_of(y, 1 - xh, e)))
    for step in (4, 5, 7, 6):
        for e in range(2):
            go(remote(w_ref.at[row_of(step), e], wbuf.at[row, core], w_send.at[step, e], w_recv.at[row, core], row_of(step), chip * 2 + e))
    for step in (1, 3, 2):
        for e in range(2):
            go(remote(w_ref.at[row_of(step), e], wbuf.at[row, core], w_send.at[step, e], w_recv.at[row, core], row_of(step), chip * 2 + e))
    for dy in (1, 3, 2):
        for e in range(2):
            go(remote(a_ref.at[e], abuf.at[col], a_send.at[dy, e], a_recv.at[col], row, col_of(y + dy, xh, e)))
    go(remote(a_ref.at[other], abuf.at[col], a_send.at[4, 0], a_recv.at[col], row, chip * 2 + other))
    go(remote(w_ref.at[row, other], wbuf.at[row, core], w_send.at[0, 0], w_recv.at[row, core], row, chip * 2 + other))
    local_a = pltpu.make_async_copy(a_ref.at[core], abuf.at[col], l_sem.at[0])
    local_w = pltpu.make_async_copy(w_ref.at[row, core], wbuf.at[row, core], l_sem.at[1])
    local_a.start()
    local_w.start()

    def arrived(buf, sem):
        pltpu.make_async_copy(buf, buf, sem).wait()

    for e in range(2):
        at = col_of(y, 1 - xh, e)
        arrived(abuf.at[at], a_recv.at[at])
        for dy in (1, 3, 2):
            go(remote(abuf.at[at], abuf.at[at], f_send.at[e, dy], a_recv.at[at], row, col_of(y + dy, xh, core)))

    local_a.wait()
    local_w.wait()
    mate = chip * 2 + other
    arrived(abuf.at[mate], a_recv.at[mate])
    arrived(wbuf.at[row, other], w_recv.at[row, other])
    for dy in (1, 3, 2):
        for xq in range(2):
            for e in range(2):
                at = col_of(y + dy, xq, e)
                arrived(abuf.at[at], a_recv.at[at])
    for step in range(1, ROWS):
        for e in range(2):
            arrived(wbuf.at[row_of(step), e], w_recv.at[row_of(step), e])

    @pl.loop(0, half)
    def _(s):
        total = jnp.zeros((4 * TILE, 4 * TILE), jnp.float32)
        for r in range(ROWS):
            left = jnp.concatenate([abuf[2 * r, s], abuf[2 * r + 1, s]], axis=1)
            right = jnp.concatenate([wbuf[r, 0, s], wbuf[r, 1, s]], axis=1)
            total = total + jnp.dot(left, right, preferred_element_type=jnp.float32)
        made = total.astype(jnp.bfloat16)
        cbuf[0, s] = made[:, :LANES]
        cbuf[1, s] = made[:, LANES:]

    pair = remote(cbuf.at[other], own_ref.at[core], c_send.at[0], c_recv.at[0], row, mate)
    go(pair)
    keep = pltpu.make_async_copy(cbuf.at[core], own_ref.at[core], l_sem.at[0])
    keep.start()

    @pl.when(jnp.logical_not(diagonal))
    def _():
        for q in range(2):
            remote(
                cbuf.at[:, :, pl.ds(q * LANES, LANES)], mir_ref.at[core], c_send.at[1 + q], c_recv.at[1 + core],
                chip, row * 2 + q,
            ).start()
        for q in range(2):
            arrived(mir_ref.at[q], c_recv.at[1 + q])
        for q in range(2):
            arrived(mir_ref.at[core], c_send.at[1 + q])

    @pl.when(diagonal)
    def _():
        there = remote(
            cbuf.at[:, :, pl.ds(other * LANES, LANES)], mir_ref.at[core], c_send.at[1], c_recv.at[1 + core], row, mate
        )
        there.start()
        here = pltpu.make_async_copy(cbuf.at[:, :, pl.ds(core * LANES, LANES)], mir_ref.at[core], c_send.at[2])
        here.start()
        arrived(mir_ref.at[other], c_recv.at[1 + other])
        there.wait_send()
        here.wait()

    keep.wait()
    arrived(own_ref.at[other], c_recv.at[0])
    for copy in started:
        copy.wait_send()


def finish(live_ref, hit_ref, at_ref, own_ref, mir_ref, mat_ref, out_ref, turn):
    slots = out_ref.shape[2]
    half = slots // 2
    lane = lax.broadcasted_iota(jnp.int32, (HALF, LANES), 1)
    low = lane < TILE

    def fold(even, odd):
        first = jnp.where(low, even, pltpu.roll(odd, TILE, 1))
        second = jnp.where(low, pltpu.roll(even, TILE, 1), odd)
        return first, second

    for s in range(slots):
        live = live_ref[s]
        hit = hit_ref[s]
        t = at_ref[s]
        for jp in range(2):
            block = mir_ref[t // half, jp, lax.rem(t, half)]
            turned = lax.dot_general(block, mat_ref[...], (((0,), (0,)), ((), ())), preferred_element_type=jnp.float32)
            turn[...] = turned * hit
            for u in range(2):
                i = jp * 2 + u
                even = turn[pl.ds(u * TILE, HALF, stride=2), :]
                odd = turn[pl.ds(u * TILE + 1, HALF, stride=2), :]
                top = own_ref[s // half, s % half, i * TILE : i * TILE + HALF, :].astype(jnp.float32)
                bottom = own_ref[s // half, s % half, i * TILE + HALF : (i + 1) * TILE, :].astype(jnp.float32)
                first, second = fold((top + even) * live, (bottom + odd) * live)
                out_ref[i, 0, s] = first
                out_ref[i, 1, s] = second


def on_device(amplitudes, integrals, pair_lists, tile_counts):
    occ_row, occ_col, slots, square = amplitudes.shape
    half = slots // 2
    tiles = integrals.shape[2]
    row = lax.axis_index("row")
    col = lax.axis_index("col")
    partner = col // 2
    bf16 = jnp.bfloat16
    vmem = pl.BlockSpec(memory_space=pltpu.VMEM)
    smem = pl.BlockSpec(memory_space=pltpu.SMEM)
    anywhere = pl.BlockSpec(memory_space=pl.ANY)

    amp = amplitudes.reshape(occ_row, occ_col, slots, HALF, LANES)
    integ = integrals.reshape(occ_row, occ_col, tiles, HALF, LANES)
    a_send = pl.pallas_call(
        pack_left,
        name="pack_left",
        out_shape=jax.ShapeDtypeStruct((2, half, occ_row * TILE, LANES), bf16),
        in_specs=[vmem, vmem],
        out_specs=vmem,
        compiler_params=pltpu.CompilerParams(vmem_limit_bytes=32 << 20),
    )(amp, jnp.asarray(merge_matrix(True), bf16))
    w_send = pl.pallas_call(
        pack_right,
        name="pack_right",
        out_shape=jax.ShapeDtypeStruct((ROWS, 2, half, occ_row * TILE, LANES), bf16),
        grid_spec=pltpu.PrefetchScalarGridSpec(
            num_scalar_prefetch=1,
            grid=(ROWS,),
            in_specs=[
                pl.BlockSpec((occ_row, occ_col, tiles, HALF, LANES), lambda r, lists: (0, 0, 0, 0, 0)),
                pl.BlockSpec((2 * LANES, 2 * LANES), lambda r, lists: (0, 0)),
            ],
            out_specs=pl.BlockSpec((1, 2, half, occ_row * TILE, LANES), lambda r, lists: (r, 0, 0, 0, 0)),
        ),
        compiler_params=pltpu.CompilerParams(vmem_limit_bytes=32 << 20),
    )(pair_lists[:, :, 1], integ, jnp.asarray(merge_matrix(False), bf16))

    own, mirror = pl.pallas_call(
        exchange,
        name="exchange",
        out_shape=(
            jax.ShapeDtypeStruct((2, half, occ_row * TILE, LANES), bf16),
            jax.ShapeDtypeStruct((2, 2, half, LANES, LANES), bf16),
        ),
        in_specs=[anywhere, anywhere],
        out_specs=(anywhere, anywhere),
        scratch_shapes=[
            pltpu.VMEM((16, half, occ_row * TILE, LANES), bf16),
            pltpu.VMEM((ROWS, 2, half, occ_row * TILE, LANES), bf16),
            pltpu.VMEM((2, half, occ_row * TILE, LANES), bf16),
            pltpu.SemaphoreType.DMA((5, 2)),
            pltpu.SemaphoreType.DMA((16,)),
            pltpu.SemaphoreType.DMA((2, 4)),
            pltpu.SemaphoreType.DMA((ROWS, 2)),
            pltpu.SemaphoreType.DMA((ROWS, 2)),
            pltpu.SemaphoreType.DMA((3,)),
            pltpu.SemaphoreType.DMA((3,)),
            pltpu.SemaphoreType.DMA((2,)),
        ],
        compiler_params=pltpu.CompilerParams(collective_id=0, has_side_effects=True, vmem_limit_bytes=40 << 20),
    )(a_send, w_send)

    mine = lax.dynamic_index_in_dim(pair_lists, row, 0, keepdims=False)
    theirs = lax.dynamic_index_in_dim(pair_lists, partner, 0, keepdims=False)
    match = (mine[:, None, 0] == theirs[None, :, 1]) & (mine[:, None, 1] == theirs[None, :, 0])
    their_live = jnp.arange(slots, dtype=jnp.int32) < tile_counts[partner]
    match = match & their_live[None, :]
    hit = jnp.any(match, axis=1).astype(jnp.float32)
    at = jnp.argmax(match, axis=1).astype(jnp.int32)
    live = (jnp.arange(slots, dtype=jnp.int32) < tile_counts[row]).astype(jnp.float32)

    packed = pl.pallas_call(
        finish,
        name="finish",
        out_shape=jax.ShapeDtypeStruct((occ_row, occ_col, slots, HALF, LANES), jnp.float32),
        in_specs=[smem, smem, smem, vmem, vmem, vmem],
        out_specs=vmem,
        scratch_shapes=[pltpu.VMEM((LANES, LANES), jnp.float32)],
        compiler_params=pltpu.CompilerParams(vmem_limit_bytes=32 << 20),
    )(live, hit, at, own, mirror, jnp.asarray(untangle_matrix(), bf16))
    return packed.reshape(occ_row, occ_col, slots, square)


def solution(mesh):
    return jax.shard_map(
        on_device,
        mesh=mesh,
        in_specs=(P("row", "col", None, None), P("row", "col", None, None), P(), P()),
        out_specs=P("row", "col", None, None),
        check_vma=False,
    )
```

```python
import functools

import jax
import jax.numpy as jnp
import numpy as np
from jax import lax
from jax.experimental import pallas as pl
from jax.experimental.pallas import tpu as pltpu
from jax.sharding import PartitionSpec as P

MESH = pl.DeviceIdType.MESH
ROWS = 8
TILE = 64
HALF = TILE // 2
LANES = 128
PHASES = 6
AHEAD = 2


def merge_matrix(permute):
    out = np.zeros((2 * LANES, 2 * LANES), np.float32)
    for operand in range(2):
        for h in range(2):
            for c in range(TILE):
                place = (c % 2) * HALF + c // 2 if permute else c
                out[operand * LANES + h * TILE + c, h * LANES + operand * TILE + place] = 1.0
    return out


def untangle_matrix():
    out = np.zeros((LANES, LANES), np.float32)
    for j in range(2):
        for h in range(2):
            for p in range(HALF):
                out[j * TILE + h * HALF + p, j * TILE + 2 * p + h] = 1.0
    return out


def exchange(
    list_ref, amp_ref, int_ref, amat_ref, wmat_ref, own_ref, mir_ref,
    a_out, w_out, abuf, wbuf, o_out, obuf, mine, cbuf, mbuf,
    a_send, a_recv, f_send, f_recv, w_send, w_recv, o_send, o_recv, p_send, p_recv, keep, m_send, m_recv, n_send, n_recv,
):
    phases, _, span = a_out.shape[:3]
    occ = amp_ref.shape[0]
    slots = amp_ref.shape[2]
    half = slots // 2
    row = lax.axis_index("row")
    col = lax.axis_index("col")
    core = lax.rem(col, 2)
    other = 1 - core
    chip = col // 2
    y = chip // 2
    z = lax.rem(row, 4)
    xh, xl = lax.rem(chip, 2), row // 4
    x = xh * 2 + xl

    def spot(x_at, y_at, z_at, core_at):
        return {"row": lax.rem(x_at, 2) * 4 + z_at, "col": (y_at * 2 + x_at // 2) * 2 + core_at}

    y1 = y + 1 - 2 * lax.rem(y, 2)
    y3 = 3 - y
    x1 = x + 1 - 2 * lax.rem(x, 2)
    z0, zt = lax.rem(z, 2), z // 2
    y0, yt = lax.rem(y, 2), y // 2
    source = yt == xl
    turn = xh != z0
    leap = jnp.logical_or(xl != yt, y0 != zt)
    leg1 = (z0 * 2 + xl, y, zt * 2 + xh)
    leg2 = (xh * 2 + yt, xl * 2 + zt, y0 * 2 + z0)

    barrier = pltpu.get_barrier_semaphore()

    def greet(place):
        pl.semaphore_signal(barrier, inc=1, device_id=place, device_id_type=MESH)

    greet(spot(x, y, z, other))
    for step in range(1, 4):
        for e in range(2):
            greet(spot(lax.rem(x + step, 4), y, z, e))
            greet(spot(x, y, lax.rem(z + step, 4), e))
    greet(spot(x, y1, z, core))
    greet(spot(x, y3, z, core))

    @pl.when(turn)
    def _():
        greet(spot(*leg1, core))

    @pl.when(leap)
    def _():
        for e in range(2):
            greet(spot(*leg2, e))

    pl.semaphore_wait(barrier, 15 + jnp.where(turn, 1, 0) + jnp.where(leap, 2, 0))

    def remote(src, dst, send, recv, place):
        return pltpu.make_async_remote_copy(
            src_ref=src, dst_ref=dst, send_sem=send, recv_sem=recv, device_id=place, device_id_type=MESH
        )

    def arrived(buf, sem):
        pltpu.make_async_copy(buf, buf, sem).wait()

    def choose(cond, yes, no):
        pl.when(cond)(yes)
        pl.when(jnp.logical_not(cond))(no)

    def pack_a():
        for i in range(occ):
            left = amp_ref[i, 0].reshape(slots * HALF, LANES)
            right = amp_ref[i, 1].reshape(slots * HALF, LANES)
            both = jnp.concatenate([left, right], axis=1)
            made = jnp.dot(both, amat_ref[...], preferred_element_type=jnp.float32).astype(jnp.bfloat16)
            for s in range(slots):
                for h in range(2):
                    a_out[s % half // span, s // half, s % span, pl.ds(i * TILE + h * HALF, HALF), :] = made[
                        s * HALF : (s + 1) * HALF, h * LANES : (h + 1) * LANES
                    ]

    def pack_w(p):
        @pl.loop(0, 8)
        def _(r):
            xi, zd = r // 4, lax.rem(r, 4)
            for e in range(2):
                for u in range(span):
                    tile = list_ref[(r * slots + e * half + p * span + u) * 2 + 1]
                    left = int_ref[:, 0, tile].reshape(occ * HALF, LANES)
                    right = int_ref[:, 1, tile].reshape(occ * HALF, LANES)
                    both = jnp.concatenate([left, right], axis=1)
                    made = jnp.dot(both, wmat_ref[...], preferred_element_type=jnp.float32).astype(jnp.bfloat16)
                    for k in range(occ):
                        for g in range(2):
                            w_out[p, zd, e, u, xi, pl.ds(k * TILE + g * HALF, HALF), :] = made[
                                k * HALF : (k + 1) * HALF, g * LANES : (g + 1) * LANES
                            ]

    def send_a(p):
        for n in range(2):
            to = yt + 2 * n
            here = abuf.at[p, y0, x, core]

            def inside(n=n, here=here):
                remote(a_out.at[p, other], here, a_send.at[p, n, 0], a_recv.at[p, x, core], spot(x, y, z, other)).start()
                pltpu.make_async_copy(a_out.at[p, core], here, a_recv.at[p, x, core]).start()

            def outside(n=n, here=here, to=to):
                for e in range(2):
                    remote(a_out.at[p, e], here, a_send.at[p, n, e], a_recv.at[p, x, core], spot(to, y, z, e)).start()

            choose(to == x, inside, outside)

    def wait_a(p):
        for n in range(2):
            arrived(a_out.at[p, 0], a_send.at[p, n, 0])

            @pl.when(yt + 2 * n != x)
            def _(n=n):
                arrived(a_out.at[p, 0], a_send.at[p, n, 1])

    def w_copies(p):
        copies = []
        for step in (1, 3, 2):
            zd = lax.rem(z + step, 4)
            for e in range(2):
                copies.append(
                    remote(w_out.at[p, zd, e], wbuf.at[p, z, core], w_send.at[p, step, e], w_recv.at[p, z, core], spot(x, y, zd, e))
                )
        copies.append(
            remote(w_out.at[p, z, other], wbuf.at[p, z, core], w_send.at[p, 0, 0], w_recv.at[p, z, core], spot(x, y, z, other))
        )
        return copies

    def send_w(p):
        for copy in w_copies(p):
            copy.start()
        pltpu.make_async_copy(w_out.at[p, z, core], wbuf.at[p, z, core], w_recv.at[p, z, core]).start()

    first = jnp.where(source, y0, 1 - y0)
    second = 1 - first

    def forward(p):
        def take():
            for xs in range(4):
                for e in range(2):
                    arrived(abuf.at[p, first, xs, e], a_recv.at[p, xs, e])

        def wait():
            arrived(abuf.at[p, first], f_recv.at[p, first])

        choose(source, take, wait)
        remote(abuf.at[p, first], abuf.at[p, first], f_send.at[p, 0], f_recv.at[p, first], spot(x, y1, z, core)).start()

        @pl.when(source)
        def _():
            remote(abuf.at[p, first], abuf.at[p, first], f_send.at[p, 1], f_recv.at[p, first], spot(x, y3, z, core)).start()

    def wait_forward(p):
        arrived(abuf.at[p, first], f_send.at[p, 0])

        @pl.when(source)
        def _():
            arrived(abuf.at[p, first], f_send.at[p, 1])

    def compute(p):
        for zs in range(4):
            for e in range(2):
                arrived(wbuf.at[p, zs, e], w_recv.at[p, zs, e])
        arrived(abuf.at[p, second], f_recv.at[p, second])
        for theirs in (True, False):
            xi = 1 - xl if theirs else xl

            @pl.loop(0, span)
            def _(u, xi=xi, theirs=theirs):
                total = jnp.zeros((4 * TILE, 4 * TILE), jnp.float32)
                for zs in range(4):
                    xs = (zs % 2) * 2 + xi
                    left = jnp.concatenate([abuf[p, zs // 2, xs, 0, u], abuf[p, zs // 2, xs, 1, u]], axis=1)
                    right = jnp.concatenate([wbuf[p, zs, 0, u, xi], wbuf[p, zs, 1, u, xi]], axis=1)
                    total = total + jnp.dot(left, right, preferred_element_type=jnp.float32)
                if theirs:
                    o_out[p, u] = total
                else:
                    mine[p, u] = total

            if theirs:
                o_copy(p).start()

    def o_copy(p):
        return remote(o_out.at[p], obuf.at[p], o_send.at[p], o_recv.at[p], spot(x1, y, z, core))

    def p_copy(p):
        return remote(cbuf.at[p, :, other], own_ref.at[core, p], p_send.at[p], p_recv.at[p], spot(x, y, z, other))

    def k_copy(p):
        return pltpu.make_async_copy(cbuf.at[p, :, core], own_ref.at[core, p], keep.at[p])

    def m_copy(p):
        return remote(cbuf.at[p], mbuf.at[p], m_send.at[p], m_recv.at[p], spot(*leg1, core))

    def n_copy(p, q, place):
        return remote(mbuf.at[p, q], mir_ref.at[core, p], n_send.at[p, q], n_recv.at[p, core], place)

    def add(p):
        arrived(obuf.at[p], o_recv.at[p])

        @pl.loop(0, span)
        def _(u):
            made = (mine[p, u] + obuf[p, u]).astype(jnp.bfloat16)
            for q in range(2):
                for j in range(2):
                    cbuf[p, q, j, u] = made[q * LANES : (q + 1) * LANES, j * LANES : (j + 1) * LANES]

        def stay():
            pltpu.make_async_copy(cbuf.at[p], mbuf.at[p], m_recv.at[p]).start()

        choose(turn, lambda: m_copy(p).start(), stay)
        p_copy(p).start()
        k_copy(p).start()

    def relay(p):
        arrived(mbuf.at[p], m_recv.at[p])

        def away():
            for q in range(2):
                n_copy(p, q, spot(*leg2, q)).start()

        def within():
            n_copy(p, other, spot(x, y, z, other)).start()
            pltpu.make_async_copy(mbuf.at[p, core], mir_ref.at[core, p], n_recv.at[p, core]).start()

        choose(leap, away, within)

    def close(p):
        for e in range(2):
            arrived(mir_ref.at[e, p], n_recv.at[p, e])
        arrived(own_ref.at[other, p], p_recv.at[p])
        k_copy(p).wait()
        p_copy(p).wait_send()
        o_copy(p).wait_send()
        pl.when(turn)(lambda: m_copy(p).wait_send())

        def away():
            for q in range(2):
                arrived(mbuf.at[p, q], n_send.at[p, q])

        def within():
            arrived(mbuf.at[p, other], n_send.at[p, other])

        choose(leap, away, within)
        wait_a(p)
        wait_forward(p)
        for copy in w_copies(p):
            copy.wait_send()

    def issue(p):
        send_a(p)
        pack_w(p)
        send_w(p)

    pack_a()
    for p in range(min(AHEAD, phases)):
        issue(p)
    forward(0)
    for p in range(phases):
        if p + AHEAD < phases:
            issue(p + AHEAD)
        if p + 1 < phases:
            forward(p + 1)
        compute(p)
        if p >= 1:
            add(p - 1)
        if p >= 2:
            relay(p - 2)
    add(phases - 1)
    if phases >= 2:
        relay(phases - 2)
    relay(phases - 1)
    for p in range(phases):
        close(p)


def finish(list_ref, count_ref, own_ref, mir_ref, mat_ref, out_ref, turn):
    slots = out_ref.shape[2]
    half = slots // 2
    span = own_ref.shape[3]
    row = lax.axis_index("row")
    partner = lax.axis_index("col") // 2
    live_count = count_ref[row]
    their_count = count_ref[partner]
    lane = lax.broadcasted_iota(jnp.int32, (HALF, LANES), 1)
    low = lane < TILE

    def fold(even, odd):
        first = jnp.where(low, even, pltpu.roll(odd, TILE, 1))
        second = jnp.where(low, pltpu.roll(even, TILE, 1), odd)
        return first, second

    @pl.loop(0, slots)
    def _(s):
        live = (s < live_count).astype(jnp.float32)
        a = list_ref[(row * slots + s) * 2]
        b = list_ref[(row * slots + s) * 2 + 1]
        found = jnp.int32(-1)
        for t in range(slots):
            same = (list_ref[(partner * slots + t) * 2] == b) & (list_ref[(partner * slots + t) * 2 + 1] == a)
            found = jnp.where(same & (t < their_count), t, found)
        hit = (found >= 0).astype(jnp.float32)
        t = jnp.maximum(found, 0)
        te, tp, tu = t // half, lax.rem(t, half) // span, lax.rem(t, span)
        se, sp, su = s // half, lax.rem(s, half) // span, lax.rem(s, span)
        for jp in range(2):
            block = mir_ref[te, tp, jp, tu]
            turned = lax.dot_general(block, mat_ref[...], (((0,), (0,)), ((), ())), preferred_element_type=jnp.float32)
            turn[...] = turned * hit
            for u in range(2):
                i = jp * 2 + u
                even = turn[pl.ds(u * TILE, HALF, stride=2), :]
                odd = turn[pl.ds(u * TILE + 1, HALF, stride=2), :]
                mine = own_ref[se, sp, jp, su]
                top = mine[u * TILE : u * TILE + HALF].astype(jnp.float32)
                bottom = mine[u * TILE + HALF : (u + 1) * TILE].astype(jnp.float32)
                first, second = fold((top + even) * live, (bottom + odd) * live)
                out_ref[i, 0, s] = first
                out_ref[i, 1, s] = second


def on_device(amplitudes, integrals, pair_lists, tile_counts):
    occ_row, occ_col, slots, square = amplitudes.shape
    half = slots // 2
    span = half // PHASES
    tiles = integrals.shape[2]
    bf16 = jnp.bfloat16
    f32 = jnp.float32
    block = occ_row * TILE
    vmem = pl.BlockSpec(memory_space=pltpu.VMEM)
    smem = pl.BlockSpec(memory_space=pltpu.SMEM)
    anywhere = pl.BlockSpec(memory_space=pl.ANY)
    dma = pltpu.SemaphoreType.DMA

    lists = pair_lists.reshape(-1)
    amp = amplitudes.reshape(occ_row, occ_col, slots, HALF, LANES)
    integ = integrals.reshape(occ_row, occ_col, tiles, HALF, LANES)

    own, mirror = pl.pallas_call(
        exchange,
        name="exchange",
        out_shape=(
            jax.ShapeDtypeStruct((2, PHASES, 2, span, LANES, LANES), bf16),
            jax.ShapeDtypeStruct((2, PHASES, 2, span, LANES, LANES), bf16),
        ),
        in_specs=[smem, vmem, vmem, vmem, vmem],
        out_specs=(anywhere, anywhere),
        scratch_shapes=[
            pltpu.VMEM((PHASES, 2, span, block, LANES), bf16),
            pltpu.VMEM((PHASES, 4, 2, span, 2, block, LANES), bf16),
            pltpu.VMEM((PHASES, 2, 4, 2, span, block, LANES), bf16),
            pltpu.VMEM((PHASES, 4, 2, span, 2, block, LANES), bf16),
            pltpu.VMEM((PHASES, span, block, 2 * LANES), f32),
            pltpu.VMEM((PHASES, span, block, 2 * LANES), f32),
            pltpu.VMEM((PHASES, span, block, 2 * LANES), f32),
            pltpu.VMEM((PHASES, 2, 2, span, LANES, LANES), bf16),
            pltpu.VMEM((PHASES, 2, 2, span, LANES, LANES), bf16),
            dma((PHASES, 2, 2)),
            dma((PHASES, 4, 2)),
            dma((PHASES, 2)),
            dma((PHASES, 2)),
            dma((PHASES, 4, 2)),
            dma((PHASES, 4, 2)),
            dma((PHASES,)),
            dma((PHASES,)),
            dma((PHASES,)),
            dma((PHASES,)),
            dma((PHASES,)),
            dma((PHASES,)),
            dma((PHASES,)),
            dma((PHASES, 2)),
            dma((PHASES, 2)),
        ],
        compiler_params=pltpu.CompilerParams(collective_id=0, has_side_effects=True, vmem_limit_bytes=48 << 20),
    )(lists, amp, integ, jnp.asarray(merge_matrix(True), bf16), jnp.asarray(merge_matrix(False), bf16))

    packed = pl.pallas_call(
        finish,
        name="finish",
        out_shape=jax.ShapeDtypeStruct((occ_row, occ_col, slots, HALF, LANES), f32),
        in_specs=[smem, smem, vmem, vmem, vmem],
        out_specs=vmem,
        scratch_shapes=[pltpu.VMEM((LANES, LANES), f32)],
        compiler_params=pltpu.CompilerParams(vmem_limit_bytes=32 << 20),
    )(lists, tile_counts, own, mirror, jnp.asarray(untangle_matrix(), bf16))
    return packed.reshape(occ_row, occ_col, slots, square)


def solution(mesh):
    return jax.shard_map(
        on_device,
        mesh=mesh,
        in_specs=(P("row", "col", None, None), P("row", "col", None, None), P(), P()),
        out_specs=P("row", "col", None, None),
        check_vma=False,
    )
```

```python
import functools

import jax
import jax.numpy as jnp
import numpy as np
from jax import lax
from jax.experimental import pallas as pl
from jax.experimental.pallas import tpu as pltpu
from jax.sharding import PartitionSpec as P

MESH = pl.DeviceIdType.MESH
ROWS = 8
TILE = 64
HALF = TILE // 2
LANES = 128
PHASES = 6
A_AHEAD = 3
W_AHEAD = 3
LAG = 2
RELAYS = (
    (0, 51, 48, 55, 5, 58, 3, 59, 7, 49, 38, 4, 11, 50, 6, 54, 18, 44, 43, 36, 42, 27, 20, 47, 24, 52, 28, 16, 46, 40, 22, 45, 23, 35, 17, 41, 34, 39, 25, 19, 29, 37, 21, 32, 31, 2, 30, 33, 13, 61, 12, 62, 9, 26, 14, 53, 8, 60, 1, 57, 10, 56, 15, 63),
    (3, 0, 5, 2, 50, 62, 53, 54, 8, 60, 48, 59, 1, 63, 6, 57, 32, 41, 44, 28, 42, 22, 29, 34, 40, 43, 16, 58, 31, 47, 46, 23, 17, 26, 38, 24, 45, 35, 7, 20, 33, 21, 25, 37, 19, 36, 18, 39, 4, 9, 14, 30, 11, 56, 15, 51, 10, 61, 49, 13, 27, 55, 12, 52),
    (14, 56, 0, 53, 62, 9, 10, 49, 59, 48, 5, 8, 3, 7, 54, 51, 21, 46, 44, 36, 57, 42, 30, 27, 20, 40, 43, 28, 17, 24, 39, 19, 29, 33, 23, 37, 16, 35, 22, 32, 25, 45, 34, 38, 18, 31, 47, 41, 26, 12, 2, 60, 6, 63, 4, 55, 13, 58, 61, 1, 52, 50, 15, 11),
    (1, 45, 8, 63, 60, 6, 53, 37, 52, 51, 4, 48, 2, 14, 49, 54, 24, 20, 19, 46, 31, 29, 35, 44, 27, 18, 58, 30, 26, 41, 25, 42, 22, 32, 10, 40, 47, 21, 38, 39, 17, 33, 16, 36, 28, 34, 23, 43, 9, 50, 61, 57, 56, 5, 12, 15, 7, 59, 62, 0, 11, 55, 13, 3),
    (8, 48, 5, 52, 6, 15, 54, 58, 4, 57, 3, 53, 14, 34, 39, 51, 63, 43, 21, 47, 25, 30, 26, 61, 37, 36, 44, 29, 40, 46, 19, 50, 17, 18, 41, 33, 27, 16, 20, 22, 45, 42, 28, 23, 35, 32, 24, 38, 2, 9, 13, 49, 56, 7, 10, 12, 31, 1, 0, 60, 55, 59, 62, 11),
    (0, 48, 4, 54, 15, 59, 7, 51, 58, 56, 3, 52, 2, 62, 57, 10, 28, 43, 24, 47, 30, 41, 27, 42, 29, 33, 18, 31, 26, 25, 34, 46, 16, 17, 20, 38, 35, 45, 40, 23, 32, 39, 37, 21, 22, 19, 36, 44, 49, 8, 1, 13, 55, 11, 63, 50, 5, 53, 9, 61, 14, 6, 60, 12),
)


def merge_matrix(permute):
    out = np.zeros((2 * LANES, 2 * LANES), np.float32)
    for operand in range(2):
        for h in range(2):
            for c in range(TILE):
                place = (c % 2) * HALF + c // 2 if permute else c
                out[operand * LANES + h * TILE + c, h * LANES + operand * TILE + place] = 1.0
    return out


def untangle_matrix():
    out = np.zeros((LANES, LANES), np.float32)
    for j in range(2):
        for h in range(2):
            for p in range(HALF):
                out[j * TILE + h * HALF + p, j * TILE + 2 * p + h] = 1.0
    return out


def exchange(
    list_ref, count_ref, amp_ref, int_ref, amat_ref, wmat_ref, own_ref, mir_ref, at_ref,
    a_out, w_out, abuf, wbuf, cbuf, mbuf,
    y_send, y_recv, x_send, v_send, v_recv, p_send, p_recv, keep, m_send, m_recv, n_send, n_recv,
):
    phases, _, span = a_out.shape[:3]
    occ = amp_ref.shape[0]
    slots = amp_ref.shape[2]
    half = slots // 2
    row = lax.axis_index("row")
    col = lax.axis_index("col")
    core = lax.rem(col, 2)
    other = 1 - core
    chip = col // 2
    y = chip // 2
    z = lax.rem(row, 4)
    xh, xl = lax.rem(chip, 2), row // 4
    x = xh * 2 + xl

    def place_of(c, core_at):
        return spot(c // 16, c // 4 % 4, c % 4, core_at)

    def spot(x_at, y_at, z_at, core_at):
        return {"row": lax.rem(x_at, 2) * 4 + z_at, "col": (y_at * 2 + x_at // 2) * 2 + core_at}

    x1 = x + 1 - 2 * lax.rem(x, 2)
    x2 = lax.rem(x + 2, 4)

    def mirror_of(c):
        xa, ya, za = c // 16, c // 4 % 4, c % 4
        return (za % 2 * 2 + ya // 2) * 16 + (xa % 2 * 2 + za // 2) * 4 + ya % 2 * 2 + xa // 2

    def look(table, at):
        value = jnp.int32(table[0])
        for n in range(1, len(table)):
            value = jnp.where(at == n, table[n], value)
        return value

    def inverse(table):
        turned = [0] * len(table)
        for n, v in enumerate(table):
            turned[v] = n
        return turned

    here = x * 16 + y * 4 + z
    goes = [look(table, here) for table in RELAYS]
    comes = [look(inverse(table), here) for table in RELAYS]
    ends = [mirror_of(c) for c in comes]
    hands = [look(table, mirror_of(here)) for table in RELAYS]

    barrier = pltpu.get_barrier_semaphore()

    def greet(place):
        pl.semaphore_signal(barrier, inc=1, device_id=place, device_id_type=MESH)

    greet(spot(x, y, z, other))
    for step in range(1, 4):
        for e in range(2):
            greet(spot(lax.rem(x + step, 4), y, z, e))
            greet(spot(x, y, lax.rem(z + step, 4), e))
    for step in range(1, 4):
        for e in range(2):
            greet(spot(x, lax.rem(y + step, 4), z, e))
            greet(spot(x1, y, lax.rem(z + step, 4), e))

    total = jnp.int32(25)
    for n in range(len(RELAYS)):
        @pl.when(comes[n] != here)
        def _(n=n):
            greet(place_of(comes[n], core))

        @pl.when(hands[n] != here)
        def _(n=n):
            for e in range(2):
                greet(place_of(hands[n], e))

        total = total + jnp.where(goes[n] != here, 1, 0) + jnp.where(ends[n] != here, 2, 0)

    pl.semaphore_wait(barrier, total)

    def remote(src, dst, send, recv, place):
        return pltpu.make_async_remote_copy(
            src_ref=src, dst_ref=dst, send_sem=send, recv_sem=recv, device_id=place, device_id_type=MESH
        )

    def arrived(buf, sem):
        pltpu.make_async_copy(buf, buf, sem).wait()

    def choose(cond, yes, no):
        pl.when(cond)(yes)
        pl.when(jnp.logical_not(cond))(no)

    def pack_a():
        for i in range(occ):
            left = amp_ref[i, 0].reshape(slots * HALF, LANES)
            right = amp_ref[i, 1].reshape(slots * HALF, LANES)
            both = jnp.concatenate([left, right], axis=1)
            made = jnp.dot(both, amat_ref[...], preferred_element_type=jnp.float32).astype(jnp.bfloat16)
            for s in range(slots):
                for h in range(2):
                    a_out[s % half // span, s // half, s % span, pl.ds(i * TILE + h * HALF, HALF), :] = made[
                        s * HALF : (s + 1) * HALF, h * LANES : (h + 1) * LANES
                    ]

    def pack_w(p):
        @pl.loop(0, 8)
        def _(r):
            xi, zd = r // 4, lax.rem(r, 4)
            for e in range(2):
                for u in range(span):
                    tile = list_ref[(r * slots + e * half + p * span + u) * 2 + 1]
                    left = int_ref[:, 0, tile].reshape(occ * HALF, LANES)
                    right = int_ref[:, 1, tile].reshape(occ * HALF, LANES)
                    both = jnp.concatenate([left, right], axis=1)
                    made = jnp.dot(both, wmat_ref[...], preferred_element_type=jnp.float32).astype(jnp.bfloat16)
                    for k in range(occ):
                        for g in range(2):
                            w_out[p, zd, e, u, xi, pl.ds(k * TILE + g * HALF, HALF), :] = made[
                                k * HALF : (k + 1) * HALF, g * LANES : (g + 1) * LANES
                            ]

    def y_copies(p):
        n = p
        here = abuf.at[p, xh, y, core]
        copies = []
        for e in range(2):
            copies.append(remote(a_out.at[p, e], here, y_send.at[n, 4, e], y_recv.at[n, xh, y, core], spot(x2, y, z, e)))
        for step in (1, 3, 2):
            for e in range(2):
                place = spot(x, lax.rem(y + step, 4), z, e)
                copies.append(remote(a_out.at[p, e], here, y_send.at[n, step, e], y_recv.at[n, xh, y, core], place))
        copies.append(remote(a_out.at[p, other], here, y_send.at[n, 0, 0], y_recv.at[n, xh, y, core], spot(x, y, z, other)))
        return copies

    def send_y(p):
        for copy in y_copies(p):
            copy.start()
        n = p
        pltpu.make_async_copy(a_out.at[p, core], abuf.at[p, xh, y, core], y_recv.at[n, xh, y, core]).start()

    def pass_copies(p):
        n = p
        copies = []
        for step in (1, 3, 2):
            for e in range(2):
                block = abuf.at[p, 1 - xh, y, e]
                place = spot(x, lax.rem(y + step, 4), z, core)
                copies.append(remote(block, block, x_send.at[n, step, e], y_recv.at[n, 1 - xh, y, e], place))
        return copies

    def pass_on(p):
        n = p
        for e in range(2):
            arrived(abuf.at[p, 1 - xh, y, e], y_recv.at[n, 1 - xh, y, e])
        for copy in pass_copies(p):
            copy.start()

    def v_copies(p):
        n = p
        copies = []
        for flip in (1, 0):
            for step in (1, 3, 2, 0):
                zd = lax.rem(z + step, 4)
                to = lax.rem(xl + flip, 2)
                for e in range(2):
                    if flip or step:
                        place = spot(xh * 2 + to, y, zd, e)
                        copies.append(
                            remote(
                                w_out.at[p, zd, e, :, to], wbuf.at[p, z, core, :, xl],
                                v_send.at[n, flip, step, e], v_recv.at[n, z, core, xl], place,
                            )
                        )
        copies.append(
            remote(
                w_out.at[p, z, other, :, xl], wbuf.at[p, z, core, :, xl],
                v_send.at[n, 0, 0, 0], v_recv.at[n, z, core, xl], spot(x, y, z, other),
            )
        )
        return copies

    def send_v(p):
        for copy in v_copies(p):
            copy.start()
        n = p
        pltpu.make_async_copy(
            w_out.at[p, z, core, :, xl], wbuf.at[p, z, core, :, xl], v_recv.at[n, z, core, xl]
        ).start()

    def compute(p):
        n = p
        for a in range(2):
            for b in range(4):
                for e in range(2):

                    @pl.when(jnp.logical_or(a == xh, b != y))
                    def _(a=a, b=b, e=e):
                        arrived(abuf.at[p, a, b, e], y_recv.at[n, a, b, e])

        for zs in range(4):
            for e in range(2):
                for ks in range(2):
                    arrived(wbuf.at[p, zs, e, :, ks], v_recv.at[n, zs, e, ks])

        @pl.loop(0, span)
        def _(u):
            total = jnp.zeros((4 * TILE, 4 * TILE), jnp.float32)
            for zs in range(4):
                for ks in range(2):
                    b = ks * 2 + zs // 2
                    left = jnp.concatenate([abuf[p, zs % 2, b, 0, u], abuf[p, zs % 2, b, 1, u]], axis=1)
                    right = jnp.concatenate([wbuf[p, zs, 0, u, ks], wbuf[p, zs, 1, u, ks]], axis=1)
                    total = total + jnp.dot(left, right, preferred_element_type=jnp.float32)
            keep_sum(p, u, total)

        emit(p)

    def p_copy(p):
        return remote(cbuf.at[p, :, other], own_ref.at[core, p], p_send.at[p], p_recv.at[p], spot(x, y, z, other))

    def k_copy(p):
        return pltpu.make_async_copy(cbuf.at[p, :, core], own_ref.at[core, p], keep.at[p])

    def m_copy(p):
        return remote(cbuf.at[p], mbuf.at[p], m_send.at[p], m_recv.at[p], place_of(goes[p % len(RELAYS)], core))

    def n_copy(p, q, place):
        return remote(mbuf.at[p, q], mir_ref.at[core, p], n_send.at[p, q], n_recv.at[p, core], place)

    def keep_sum(p, u, total):
        made = total.astype(jnp.bfloat16)
        for q in range(2):
            for j in range(2):
                cbuf[p, q, j, u] = made[q * LANES : (q + 1) * LANES, j * LANES : (j + 1) * LANES]

    def emit(p):
        def stay():
            pltpu.make_async_copy(cbuf.at[p], mbuf.at[p], m_recv.at[p]).start()

        choose(goes[p % len(RELAYS)] != here, lambda: m_copy(p).start(), stay)
        p_copy(p).start()
        k_copy(p).start()

    def relay(p):
        arrived(mbuf.at[p], m_recv.at[p])

        def away():
            for q in range(2):
                n_copy(p, q, place_of(ends[p % len(RELAYS)], q)).start()

        def within():
            n_copy(p, other, spot(x, y, z, other)).start()
            pltpu.make_async_copy(mbuf.at[p, core], mir_ref.at[core, p], n_recv.at[p, core]).start()

        choose(ends[p % len(RELAYS)] != here, away, within)

    def close(p):
        for e in range(2):
            arrived(mir_ref.at[e, p], n_recv.at[p, e])
        arrived(own_ref.at[other, p], p_recv.at[p])
        k_copy(p).wait()
        p_copy(p).wait_send()
        pl.when(goes[p % len(RELAYS)] != here)(lambda: m_copy(p).wait_send())

        def away():
            for q in range(2):
                arrived(mbuf.at[p, q], n_send.at[p, q])

        def within():
            arrived(mbuf.at[p, other], n_send.at[p, other])

        choose(ends[p % len(RELAYS)] != here, away, within)
        for copy in y_copies(p) + pass_copies(p) + v_copies(p):
            copy.wait_send()

    def find():
        for s in range(slots):
            a = list_ref[(row * slots + s) * 2]
            b = list_ref[(row * slots + s) * 2 + 1]
            found = jnp.int32(-1)
            for t in range(slots):
                same = (list_ref[(chip * slots + t) * 2] == b) & (list_ref[(chip * slots + t) * 2 + 1] == a)
                found = jnp.where(same & (t < count_ref[chip]), t, found)
            at_ref[0, s] = jnp.maximum(found, 0)
            at_ref[1, s] = (found >= 0).astype(jnp.int32)
            at_ref[2, s] = (s < count_ref[row]).astype(jnp.int32)

    pack_a()
    for p in range(min(A_AHEAD, phases)):
        send_y(p)
    for p in range(min(W_AHEAD, phases)):
        pack_w(p)
        send_v(p)
        if p == 0:
            pass_on(0)
    find()
    for p in range(phases):
        if p + A_AHEAD < phases:
            send_y(p + A_AHEAD)
        if p + 1 < phases:
            pass_on(p + 1)
        if p + W_AHEAD < phases:
            pack_w(p + W_AHEAD)
            send_v(p + W_AHEAD)
        compute(p)
        if p >= LAG:
            relay(p - LAG)
    for p in range(max(phases - LAG, 0), phases):
        relay(p)
    for p in range(phases):
        close(p)


def finish(at_ref, own_ref, mir_ref, mat_ref, out_ref, turn):
    slots = out_ref.shape[2]
    half = slots // 2
    span = own_ref.shape[3]
    lane = lax.broadcasted_iota(jnp.int32, (HALF, LANES), 1)
    low = lane < TILE

    def fold(even, odd):
        first = jnp.where(low, even, pltpu.roll(odd, TILE, 1))
        second = jnp.where(low, pltpu.roll(even, TILE, 1), odd)
        return first, second

    for s in range(slots):
        t = at_ref[0, s]
        hit = at_ref[1, s].astype(jnp.float32)
        live = at_ref[2, s].astype(jnp.float32)
        te, tp, tu = t // half, lax.rem(t, half) // span, lax.rem(t, span)
        se, sp, su = s // half, s % half // span, s % span
        for jp in range(2):
            block = mir_ref[te, tp, jp, tu]
            turned = lax.dot_general(block, mat_ref[...], (((0,), (0,)), ((), ())), preferred_element_type=jnp.float32)
            turn[s % 2, jp] = turned * hit
            mine = own_ref[se, sp, jp, su].astype(jnp.float32)
            for u in range(2):
                i = jp * 2 + u
                even = turn[s % 2, jp, pl.ds(u * TILE, HALF, stride=2), :]
                odd = turn[s % 2, jp, pl.ds(u * TILE + 1, HALF, stride=2), :]
                top = mine[u * TILE : u * TILE + HALF]
                bottom = mine[u * TILE + HALF : (u + 1) * TILE]
                first, second = fold((top + even) * live, (bottom + odd) * live)
                out_ref[i, 0, s] = first
                out_ref[i, 1, s] = second


def on_device(amplitudes, integrals, pair_lists, tile_counts):
    occ_row, occ_col, slots, square = amplitudes.shape
    half = slots // 2
    span = half // PHASES
    tiles = integrals.shape[2]
    bf16 = jnp.bfloat16
    f32 = jnp.float32
    block = occ_row * TILE
    vmem = pl.BlockSpec(memory_space=pltpu.VMEM)
    smem = pl.BlockSpec(memory_space=pltpu.SMEM)
    anywhere = pl.BlockSpec(memory_space=pl.ANY)
    dma = pltpu.SemaphoreType.DMA

    lists = pair_lists.reshape(-1)
    amp = amplitudes.reshape(occ_row, occ_col, slots, HALF, LANES)
    integ = integrals.reshape(occ_row, occ_col, tiles, HALF, LANES)

    own, mirror, places = pl.pallas_call(
        exchange,
        name="exchange",
        out_shape=(
            jax.ShapeDtypeStruct((2, PHASES, 2, span, LANES, LANES), bf16),
            jax.ShapeDtypeStruct((2, PHASES, 2, span, LANES, LANES), bf16),
            jax.ShapeDtypeStruct((3, slots), jnp.int32),
        ),
        in_specs=[smem, smem, vmem, vmem, vmem, vmem],
        out_specs=(anywhere, anywhere, smem),
        scratch_shapes=[
            pltpu.VMEM((PHASES, 2, span, block, LANES), bf16),
            pltpu.VMEM((PHASES, 4, 2, span, 2, block, LANES), bf16),
            pltpu.VMEM((PHASES, 2, 4, 2, span, block, LANES), bf16),
            pltpu.VMEM((PHASES, 4, 2, span, 2, block, LANES), bf16),
            pltpu.VMEM((PHASES, 2, 2, span, LANES, LANES), bf16),
            pltpu.VMEM((PHASES, 2, 2, span, LANES, LANES), bf16),
            dma((PHASES, 5, 2)),
            dma((PHASES, 2, 4, 2)),
            dma((PHASES, 4, 2)),
            dma((PHASES, 2, 4, 2)),
            dma((PHASES, 4, 2, 2)),
            dma((PHASES,)),
            dma((PHASES,)),
            dma((PHASES,)),
            dma((PHASES,)),
            dma((PHASES,)),
            dma((PHASES, 2)),
            dma((PHASES, 2)),
        ],
        compiler_params=pltpu.CompilerParams(collective_id=0, has_side_effects=True, vmem_limit_bytes=48 << 20),
    )(lists, tile_counts, amp, integ, jnp.asarray(merge_matrix(True), bf16), jnp.asarray(merge_matrix(False), bf16))

    packed = pl.pallas_call(
        finish,
        name="finish",
        out_shape=jax.ShapeDtypeStruct((occ_row, occ_col, slots, HALF, LANES), f32),
        in_specs=[smem, vmem, vmem, vmem],
        out_specs=vmem,
        scratch_shapes=[pltpu.VMEM((2, 2, LANES, LANES), f32)],
        compiler_params=pltpu.CompilerParams(vmem_limit_bytes=32 << 20),
    )(places, own, mirror, jnp.asarray(untangle_matrix(), bf16))
    return packed.reshape(occ_row, occ_col, slots, square)


def solution(mesh):
    return jax.shard_map(
        on_device,
        mesh=mesh,
        in_specs=(P("row", "col", None, None), P("row", "col", None, None), P(), P()),
        out_specs=P("row", "col", None, None),
        check_vma=False,
    )
```

```python
import functools

import jax
import jax.numpy as jnp
import numpy as np
from jax import lax
from jax.experimental import pallas as pl
from jax.experimental.pallas import tpu as pltpu
from jax.sharding import PartitionSpec as P

MESH = pl.DeviceIdType.MESH
ROWS = 8
TILE = 64
HALF = TILE // 2
LANES = 128
PHASES = 6
A_AHEAD = 3
W_AHEAD = 3
LAG = 2
RELAYS = (
    (0, 51, 48, 55, 5, 58, 3, 59, 7, 49, 38, 4, 11, 50, 6, 54, 18, 44, 43, 36, 42, 27, 20, 47, 24, 52, 28, 16, 46, 40, 22, 45, 23, 35, 17, 41, 34, 39, 25, 19, 29, 37, 21, 32, 31, 2, 30, 33, 13, 61, 12, 62, 9, 26, 14, 53, 8, 60, 1, 57, 10, 56, 15, 63),
    (3, 0, 5, 2, 50, 62, 53, 54, 8, 60, 48, 59, 1, 63, 6, 57, 32, 41, 44, 28, 42, 22, 29, 34, 40, 43, 16, 58, 31, 47, 46, 23, 17, 26, 38, 24, 45, 35, 7, 20, 33, 21, 25, 37, 19, 36, 18, 39, 4, 9, 14, 30, 11, 56, 15, 51, 10, 61, 49, 13, 27, 55, 12, 52),
    (14, 56, 0, 53, 62, 9, 10, 49, 59, 48, 5, 8, 3, 7, 54, 51, 21, 46, 44, 36, 57, 42, 30, 27, 20, 40, 43, 28, 17, 24, 39, 19, 29, 33, 23, 37, 16, 35, 22, 32, 25, 45, 34, 38, 18, 31, 47, 41, 26, 12, 2, 60, 6, 63, 4, 55, 13, 58, 61, 1, 52, 50, 15, 11),
    (1, 45, 8, 63, 60, 6, 53, 37, 52, 51, 4, 48, 2, 14, 49, 54, 24, 20, 19, 46, 31, 29, 35, 44, 27, 18, 58, 30, 26, 41, 25, 42, 22, 32, 10, 40, 47, 21, 38, 39, 17, 33, 16, 36, 28, 34, 23, 43, 9, 50, 61, 57, 56, 5, 12, 15, 7, 59, 62, 0, 11, 55, 13, 3),
    (8, 48, 5, 52, 6, 15, 54, 58, 4, 57, 3, 53, 14, 34, 39, 51, 63, 43, 21, 47, 25, 30, 26, 61, 37, 36, 44, 29, 40, 46, 19, 50, 17, 18, 41, 33, 27, 16, 20, 22, 45, 42, 28, 23, 35, 32, 24, 38, 2, 9, 13, 49, 56, 7, 10, 12, 31, 1, 0, 60, 55, 59, 62, 11),
    (0, 48, 4, 54, 15, 59, 7, 51, 58, 56, 3, 52, 2, 62, 57, 10, 28, 43, 24, 47, 30, 41, 27, 42, 29, 33, 18, 31, 26, 25, 34, 46, 16, 17, 20, 38, 35, 45, 40, 23, 32, 39, 37, 21, 22, 19, 36, 44, 49, 8, 1, 13, 55, 11, 63, 50, 5, 53, 9, 61, 14, 6, 60, 12),
)


def merge_matrix(permute):
    out = np.zeros((2 * LANES, 2 * LANES), np.float32)
    for operand in range(2):
        for h in range(2):
            for c in range(TILE):
                place = (c % 2) * HALF + c // 2 if permute else c
                out[operand * LANES + h * TILE + c, h * LANES + operand * TILE + place] = 1.0
    return out


def untangle_matrix():
    out = np.zeros((LANES, LANES), np.float32)
    for j in range(2):
        for h in range(2):
            for p in range(HALF):
                out[j * TILE + h * HALF + p, j * TILE + 2 * p + h] = 1.0
    return out


def exchange(
    list_ref, count_ref, amp_ref, int_ref, amat_ref, wmat_ref, own_ref, mir_ref, at_ref,
    a_out, w_out, abuf, wbuf, cbuf, mbuf, wide,
    y_send, y_recv, x_send, v_send, v_recv, p_send, p_recv, keep, m_send, m_recv, n_send, n_recv,
):
    phases, _, span = a_out.shape[:3]
    occ = amp_ref.shape[0]
    slots = amp_ref.shape[1]
    half = slots // 2
    row = lax.axis_index("row")
    col = lax.axis_index("col")
    core = lax.rem(col, 2)
    other = 1 - core
    chip = col // 2
    y = chip // 2
    z = lax.rem(row, 4)
    xh, xl = lax.rem(chip, 2), row // 4
    x = xh * 2 + xl

    def place_of(c, core_at):
        return spot(c // 16, c // 4 % 4, c % 4, core_at)

    def spot(x_at, y_at, z_at, core_at):
        return {"row": lax.rem(x_at, 2) * 4 + z_at, "col": (y_at * 2 + x_at // 2) * 2 + core_at}

    x1 = x + 1 - 2 * lax.rem(x, 2)
    x2 = lax.rem(x + 2, 4)

    def mirror_of(c):
        xa, ya, za = c // 16, c // 4 % 4, c % 4
        return (za % 2 * 2 + ya // 2) * 16 + (xa % 2 * 2 + za // 2) * 4 + ya % 2 * 2 + xa // 2

    def look(table, at):
        value = jnp.int32(table[0])
        for n in range(1, len(table)):
            value = jnp.where(at == n, table[n], value)
        return value

    def inverse(table):
        turned = [0] * len(table)
        for n, v in enumerate(table):
            turned[v] = n
        return turned

    here = x * 16 + y * 4 + z
    goes = [look(table, here) for table in RELAYS]
    comes = [look(inverse(table), here) for table in RELAYS]
    ends = [mirror_of(c) for c in comes]
    hands = [look(table, mirror_of(here)) for table in RELAYS]

    barrier = pltpu.get_barrier_semaphore()

    def greet(place):
        pl.semaphore_signal(barrier, inc=1, device_id=place, device_id_type=MESH)

    greet(spot(x, y, z, other))
    for step in range(1, 4):
        for e in range(2):
            greet(spot(lax.rem(x + step, 4), y, z, e))
            greet(spot(x, y, lax.rem(z + step, 4), e))
    for step in range(1, 4):
        for e in range(2):
            greet(spot(x, lax.rem(y + step, 4), z, e))
            greet(spot(x1, y, lax.rem(z + step, 4), e))

    total = jnp.int32(25)
    for n in range(len(RELAYS)):
        @pl.when(comes[n] != here)
        def _(n=n):
            greet(place_of(comes[n], core))

        @pl.when(hands[n] != here)
        def _(n=n):
            for e in range(2):
                greet(place_of(hands[n], e))

        total = total + jnp.where(goes[n] != here, 1, 0) + jnp.where(ends[n] != here, 2, 0)

    pl.semaphore_wait(barrier, total)

    def remote(src, dst, send, recv, place):
        return pltpu.make_async_remote_copy(
            src_ref=src, dst_ref=dst, send_sem=send, recv_sem=recv, device_id=place, device_id_type=MESH
        )

    def arrived(buf, sem):
        pltpu.make_async_copy(buf, buf, sem).wait()

    def choose(cond, yes, no):
        pl.when(cond)(yes)
        pl.when(jnp.logical_not(cond))(no)

    def pack_a():
        for i in range(occ):
            wide[...] = amp_ref[i].reshape(slots * TILE, LANES).astype(jnp.float32)
            left = wide[pl.ds(0, slots * HALF, stride=2), :].astype(jnp.bfloat16)
            right = wide[pl.ds(1, slots * HALF, stride=2), :].astype(jnp.bfloat16)
            both = jnp.concatenate([left, right], axis=1)
            made = jnp.dot(both, amat_ref[...], preferred_element_type=jnp.float32).astype(jnp.bfloat16)
            for s in range(slots):
                for h in range(2):
                    a_out[s % half // span, s // half, s % span, pl.ds(i * TILE + h * HALF, HALF), :] = made[
                        s * HALF : (s + 1) * HALF, h * LANES : (h + 1) * LANES
                    ]

    def pack_w(p):
        @pl.loop(0, 8)
        def _(r):
            xi, zd = r // 4, lax.rem(r, 4)
            for e in range(2):
                for u in range(span):
                    tile = list_ref[(r * slots + e * half + p * span + u) * 2 + 1]
                    at = (e * span + u) * occ * TILE
                    wide[pl.ds(at, occ * TILE), :] = int_ref[:, tile].reshape(occ * TILE, LANES).astype(jnp.float32)
                    left = wide[pl.ds(at, occ * HALF, stride=2), :].astype(jnp.bfloat16)
                    right = wide[pl.ds(at + 1, occ * HALF, stride=2), :].astype(jnp.bfloat16)
                    both = jnp.concatenate([left, right], axis=1)
                    made = jnp.dot(both, wmat_ref[...], preferred_element_type=jnp.float32).astype(jnp.bfloat16)
                    for k in range(occ):
                        for g in range(2):
                            w_out[p, zd, e, u, xi, pl.ds(k * TILE + g * HALF, HALF), :] = made[
                                k * HALF : (k + 1) * HALF, g * LANES : (g + 1) * LANES
                            ]

    def y_copies(p):
        n = p
        here = abuf.at[p, xh, y, core]
        copies = []
        for e in range(2):
            copies.append(remote(a_out.at[p, e], here, y_send.at[n, 4, e], y_recv.at[n, xh, y, core], spot(x2, y, z, e)))
        for step in (1, 3, 2):
            for e in range(2):
                place = spot(x, lax.rem(y + step, 4), z, e)
                copies.append(remote(a_out.at[p, e], here, y_send.at[n, step, e], y_recv.at[n, xh, y, core], place))
        copies.append(remote(a_out.at[p, other], here, y_send.at[n, 0, 0], y_recv.at[n, xh, y, core], spot(x, y, z, other)))
        return copies

    def send_y(p):
        for copy in y_copies(p):
            copy.start()
        n = p
        pltpu.make_async_copy(a_out.at[p, core], abuf.at[p, xh, y, core], y_recv.at[n, xh, y, core]).start()

    def pass_copies(p):
        n = p
        copies = []
        for step in (1, 3, 2):
            for e in range(2):
                block = abuf.at[p, 1 - xh, y, e]
                place = spot(x, lax.rem(y + step, 4), z, core)
                copies.append(remote(block, block, x_send.at[n, step, e], y_recv.at[n, 1 - xh, y, e], place))
        return copies

    def pass_on(p):
        n = p
        for e in range(2):
            arrived(abuf.at[p, 1 - xh, y, e], y_recv.at[n, 1 - xh, y, e])
        for copy in pass_copies(p):
            copy.start()

    def v_copies(p):
        n = p
        copies = []
        for flip in (1, 0):
            for step in (1, 3, 2, 0):
                zd = lax.rem(z + step, 4)
                to = lax.rem(xl + flip, 2)
                for e in range(2):
                    if flip or step:
                        place = spot(xh * 2 + to, y, zd, e)
                        copies.append(
                            remote(
                                w_out.at[p, zd, e, :, to], wbuf.at[p, z, core, :, xl],
                                v_send.at[n, flip, step, e], v_recv.at[n, z, core, xl], place,
                            )
                        )
        copies.append(
            remote(
                w_out.at[p, z, other, :, xl], wbuf.at[p, z, core, :, xl],
                v_send.at[n, 0, 0, 0], v_recv.at[n, z, core, xl], spot(x, y, z, other),
            )
        )
        return copies

    def send_v(p):
        for copy in v_copies(p):
            copy.start()
        n = p
        pltpu.make_async_copy(
            w_out.at[p, z, core, :, xl], wbuf.at[p, z, core, :, xl], v_recv.at[n, z, core, xl]
        ).start()

    def compute(p):
        n = p
        for a in range(2):
            for b in range(4):
                for e in range(2):

                    @pl.when(jnp.logical_or(a == xh, b != y))
                    def _(a=a, b=b, e=e):
                        arrived(abuf.at[p, a, b, e], y_recv.at[n, a, b, e])

        for zs in range(4):
            for e in range(2):
                for ks in range(2):
                    arrived(wbuf.at[p, zs, e, :, ks], v_recv.at[n, zs, e, ks])

        @pl.loop(0, span)
        def _(u):
            total = jnp.zeros((4 * TILE, 4 * TILE), jnp.float32)
            for zs in range(4):
                for ks in range(2):
                    b = ks * 2 + zs // 2
                    left = jnp.concatenate([abuf[p, zs % 2, b, 0, u], abuf[p, zs % 2, b, 1, u]], axis=1)
                    right = jnp.concatenate([wbuf[p, zs, 0, u, ks], wbuf[p, zs, 1, u, ks]], axis=1)
                    total = total + jnp.dot(left, right, preferred_element_type=jnp.float32)
            keep_sum(p, u, total)

        emit(p)

    def p_copy(p):
        return remote(cbuf.at[p, :, other], own_ref.at[core, p], p_send.at[p], p_recv.at[p], spot(x, y, z, other))

    def k_copy(p):
        return pltpu.make_async_copy(cbuf.at[p, :, core], own_ref.at[core, p], keep.at[p])

    def m_copy(p):
        return remote(cbuf.at[p], mbuf.at[p], m_send.at[p], m_recv.at[p], place_of(goes[p % len(RELAYS)], core))

    def n_copy(p, q, place):
        return remote(mbuf.at[p, q], mir_ref.at[core, p], n_send.at[p, q], n_recv.at[p, core], place)

    def keep_sum(p, u, total):
        made = total.astype(jnp.bfloat16)
        for q in range(2):
            for j in range(2):
                cbuf[p, q, j, u] = made[q * LANES : (q + 1) * LANES, j * LANES : (j + 1) * LANES]

    def emit(p):
        def stay():
            pltpu.make_async_copy(cbuf.at[p], mbuf.at[p], m_recv.at[p]).start()

        choose(goes[p % len(RELAYS)] != here, lambda: m_copy(p).start(), stay)
        p_copy(p).start()
        k_copy(p).start()

    def relay(p):
        arrived(mbuf.at[p], m_recv.at[p])

        def away():
            for q in range(2):
                n_copy(p, q, place_of(ends[p % len(RELAYS)], q)).start()

        def within():
            n_copy(p, other, spot(x, y, z, other)).start()
            pltpu.make_async_copy(mbuf.at[p, core], mir_ref.at[core, p], n_recv.at[p, core]).start()

        choose(ends[p % len(RELAYS)] != here, away, within)

    def close(p):
        for e in range(2):
            arrived(mir_ref.at[e, p], n_recv.at[p, e])
        arrived(own_ref.at[other, p], p_recv.at[p])
        k_copy(p).wait()
        p_copy(p).wait_send()
        pl.when(goes[p % len(RELAYS)] != here)(lambda: m_copy(p).wait_send())

        def away():
            for q in range(2):
                arrived(mbuf.at[p, q], n_send.at[p, q])

        def within():
            arrived(mbuf.at[p, other], n_send.at[p, other])

        choose(ends[p % len(RELAYS)] != here, away, within)
        for copy in y_copies(p) + pass_copies(p) + v_copies(p):
            copy.wait_send()

    def find():
        for s in range(slots):
            a = list_ref[(row * slots + s) * 2]
            b = list_ref[(row * slots + s) * 2 + 1]
            found = jnp.int32(-1)
            for t in range(slots):
                same = (list_ref[(chip * slots + t) * 2] == b) & (list_ref[(chip * slots + t) * 2 + 1] == a)
                found = jnp.where(same & (t < count_ref[chip]), t, found)
            at_ref[0, s] = jnp.maximum(found, 0)
            at_ref[1, s] = (found >= 0).astype(jnp.int32)
            at_ref[2, s] = (s < count_ref[row]).astype(jnp.int32)

    pack_a()
    for p in range(min(A_AHEAD, phases)):
        send_y(p)
    for p in range(min(W_AHEAD, phases)):
        pack_w(p)
        send_v(p)
        if p == 0:
            pass_on(0)
    find()
    for p in range(phases):
        if p + A_AHEAD < phases:
            send_y(p + A_AHEAD)
        if p + 1 < phases:
            pass_on(p + 1)
        if p + W_AHEAD < phases:
            pack_w(p + W_AHEAD)
            send_v(p + W_AHEAD)
        compute(p)
        if p >= LAG:
            relay(p - LAG)
    for p in range(max(phases - LAG, 0), phases):
        relay(p)
    for p in range(phases):
        close(p)


def finish(at_ref, own_ref, mir_ref, mat_ref, out_ref, turn):
    slots = out_ref.shape[1]
    half = slots // 2
    span = own_ref.shape[3]
    lane = lax.broadcasted_iota(jnp.int32, (HALF, LANES), 1)
    low = lane < TILE

    def fold(even, odd):
        first = jnp.where(low, even, pltpu.roll(odd, TILE, 1))
        second = jnp.where(low, pltpu.roll(even, TILE, 1), odd)
        return first, second

    for s in range(slots):
        t = at_ref[0, s]
        hit = at_ref[1, s].astype(jnp.float32)
        live = at_ref[2, s].astype(jnp.float32)
        te, tp, tu = t // half, lax.rem(t, half) // span, lax.rem(t, span)
        se, sp, su = s // half, s % half // span, s % span
        for jp in range(2):
            block = mir_ref[te, tp, jp, tu]
            turned = lax.dot_general(block, mat_ref[...], (((0,), (0,)), ((), ())), preferred_element_type=jnp.float32)
            turn[s % 2, jp] = turned * hit
            mine = own_ref[se, sp, jp, su].astype(jnp.float32)
            for u in range(2):
                i = jp * 2 + u
                even = turn[s % 2, jp, pl.ds(u * TILE, HALF, stride=2), :]
                odd = turn[s % 2, jp, pl.ds(u * TILE + 1, HALF, stride=2), :]
                top = mine[u * TILE : u * TILE + HALF]
                bottom = mine[u * TILE + HALF : (u + 1) * TILE]
                first, second = fold((top + even) * live, (bottom + odd) * live)
                out_ref[i, s, pl.ds(0, HALF, stride=2), :] = first
                out_ref[i, s, pl.ds(1, HALF, stride=2), :] = second


def on_device(amplitudes, integrals, pair_lists, tile_counts):
    occ_row, occ_col, slots, square = amplitudes.shape
    half = slots // 2
    span = half // PHASES
    tiles = integrals.shape[2]
    bf16 = jnp.bfloat16
    f32 = jnp.float32
    block = occ_row * TILE
    vmem = pl.BlockSpec(memory_space=pltpu.VMEM)
    smem = pl.BlockSpec(memory_space=pltpu.SMEM)
    anywhere = pl.BlockSpec(memory_space=pl.ANY)
    dma = pltpu.SemaphoreType.DMA

    lists = pair_lists.reshape(-1)
    amp = amplitudes.reshape(occ_row, occ_col, slots, HALF, LANES).transpose(0, 2, 3, 1, 4)
    amp = amp.reshape(occ_row, slots, TILE, LANES)
    integ = integrals.reshape(occ_row, occ_col, tiles, HALF, LANES).transpose(0, 2, 3, 1, 4)
    integ = integ.reshape(occ_row, tiles, TILE, LANES)

    own, mirror, places = pl.pallas_call(
        exchange,
        name="exchange",
        out_shape=(
            jax.ShapeDtypeStruct((2, PHASES, 2, span, LANES, LANES), bf16),
            jax.ShapeDtypeStruct((2, PHASES, 2, span, LANES, LANES), bf16),
            jax.ShapeDtypeStruct((3, slots), jnp.int32),
        ),
        in_specs=[smem, smem, vmem, vmem, vmem, vmem],
        out_specs=(anywhere, anywhere, smem),
        scratch_shapes=[
            pltpu.VMEM((PHASES, 2, span, block, LANES), bf16),
            pltpu.VMEM((PHASES, 4, 2, span, 2, block, LANES), bf16),
            pltpu.VMEM((PHASES, 2, 4, 2, span, block, LANES), bf16),
            pltpu.VMEM((PHASES, 4, 2, span, 2, block, LANES), bf16),
            pltpu.VMEM((PHASES, 2, 2, span, LANES, LANES), bf16),
            pltpu.VMEM((PHASES, 2, 2, span, LANES, LANES), bf16),
            pltpu.VMEM((max(slots * TILE, 2 * span * block), LANES), f32),
            dma((PHASES, 5, 2)),
            dma((PHASES, 2, 4, 2)),
            dma((PHASES, 4, 2)),
            dma((PHASES, 2, 4, 2)),
            dma((PHASES, 4, 2, 2)),
            dma((PHASES,)),
            dma((PHASES,)),
            dma((PHASES,)),
            dma((PHASES,)),
            dma((PHASES,)),
            dma((PHASES, 2)),
            dma((PHASES, 2)),
        ],
        compiler_params=pltpu.CompilerParams(collective_id=0, has_side_effects=True, vmem_limit_bytes=48 << 20),
    )(lists, tile_counts, amp, integ, jnp.asarray(merge_matrix(True), bf16), jnp.asarray(merge_matrix(False), bf16))

    packed = pl.pallas_call(
        finish,
        name="finish",
        out_shape=jax.ShapeDtypeStruct((occ_row, slots, TILE, LANES), f32),
        in_specs=[smem, vmem, vmem, vmem],
        out_specs=vmem,
        scratch_shapes=[pltpu.VMEM((2, 2, LANES, LANES), f32)],
        compiler_params=pltpu.CompilerParams(vmem_limit_bytes=32 << 20),
    )(places, own, mirror, jnp.asarray(untangle_matrix(), bf16))
    packed = packed.reshape(occ_row, slots, HALF, occ_col, LANES).transpose(0, 3, 1, 2, 4)
    return packed.reshape(occ_row, occ_col, slots, square)


def solution(mesh):
    return jax.shard_map(
        on_device,
        mesh=mesh,
        in_specs=(P("row", "col", None, None), P("row", "col", None, None), P(), P()),
        out_specs=P("row", "col", None, None),
        check_vma=False,
    )
```

```python
import functools

import jax
import jax.numpy as jnp
import numpy as np
from jax import lax
from jax.experimental import pallas as pl
from jax.experimental.pallas import tpu as pltpu
from jax.sharding import PartitionSpec as P

MESH = pl.DeviceIdType.MESH
ROWS = 8
TILE = 64
HALF = TILE // 2
LANES = 128
PHASES = 6
A_AHEAD = 2
W_AHEAD = 2
LAG = 2
RELAYS = (
    (0, 51, 48, 55, 5, 58, 3, 59, 7, 49, 38, 4, 11, 50, 6, 54, 18, 44, 43, 36, 42, 27, 20, 47, 24, 52, 28, 16, 46, 40, 22, 45, 23, 35, 17, 41, 34, 39, 25, 19, 29, 37, 21, 32, 31, 2, 30, 33, 13, 61, 12, 62, 9, 26, 14, 53, 8, 60, 1, 57, 10, 56, 15, 63),
    (3, 0, 5, 2, 50, 62, 53, 54, 8, 60, 48, 59, 1, 63, 6, 57, 32, 41, 44, 28, 42, 22, 29, 34, 40, 43, 16, 58, 31, 47, 46, 23, 17, 26, 38, 24, 45, 35, 7, 20, 33, 21, 25, 37, 19, 36, 18, 39, 4, 9, 14, 30, 11, 56, 15, 51, 10, 61, 49, 13, 27, 55, 12, 52),
    (14, 56, 0, 53, 62, 9, 10, 49, 59, 48, 5, 8, 3, 7, 54, 51, 21, 46, 44, 36, 57, 42, 30, 27, 20, 40, 43, 28, 17, 24, 39, 19, 29, 33, 23, 37, 16, 35, 22, 32, 25, 45, 34, 38, 18, 31, 47, 41, 26, 12, 2, 60, 6, 63, 4, 55, 13, 58, 61, 1, 52, 50, 15, 11),
    (1, 45, 8, 63, 60, 6, 53, 37, 52, 51, 4, 48, 2, 14, 49, 54, 24, 20, 19, 46, 31, 29, 35, 44, 27, 18, 58, 30, 26, 41, 25, 42, 22, 32, 10, 40, 47, 21, 38, 39, 17, 33, 16, 36, 28, 34, 23, 43, 9, 50, 61, 57, 56, 5, 12, 15, 7, 59, 62, 0, 11, 55, 13, 3),
    (8, 48, 5, 52, 6, 15, 54, 58, 4, 57, 3, 53, 14, 34, 39, 51, 63, 43, 21, 47, 25, 30, 26, 61, 37, 36, 44, 29, 40, 46, 19, 50, 17, 18, 41, 33, 27, 16, 20, 22, 45, 42, 28, 23, 35, 32, 24, 38, 2, 9, 13, 49, 56, 7, 10, 12, 31, 1, 0, 60, 55, 59, 62, 11),
    (0, 48, 4, 54, 15, 59, 7, 51, 58, 56, 3, 52, 2, 62, 57, 10, 28, 43, 24, 47, 30, 41, 27, 42, 29, 33, 18, 31, 26, 25, 34, 46, 16, 17, 20, 38, 35, 45, 40, 23, 32, 39, 37, 21, 22, 19, 36, 44, 49, 8, 1, 13, 55, 11, 63, 50, 5, 53, 9, 61, 14, 6, 60, 12),
)


def merge_matrix(permute):
    row = lax.broadcasted_iota(jnp.int32, (2 * LANES, 2 * LANES), 0)
    col = lax.broadcasted_iota(jnp.int32, (2 * LANES, 2 * LANES), 1)
    c = row & (TILE - 1)
    place = (c & 1) * HALF + (c >> 1) if permute else c
    target = ((row >> 6) & 1) * LANES + (row >> 7) * TILE + place
    return jnp.where(col == target, 1.0, 0.0).astype(jnp.bfloat16)


def untangle_matrix():
    out = np.zeros((LANES, LANES), np.float32)
    for j in range(2):
        for h in range(2):
            for p in range(HALF):
                out[j * TILE + h * HALF + p, j * TILE + 2 * p + h] = 1.0
    return out


def exchange(
    list_ref, count_ref, amp_any, int_any, own_ref, mir_ref, at_ref,
    amp_ref, int_ref, amat_ref, wmat_ref, a_out, w_out, abuf, wbuf, cbuf, mbuf, wide, load,
    y_send, y_recv, x_send, v_send, v_recv, p_send, p_recv, keep, m_send, m_recv, n_send, n_recv,
):
    phases, _, span = a_out.shape[:3]
    amp_load = pltpu.make_async_copy(amp_any, amp_ref, load.at[0])
    int_load = pltpu.make_async_copy(int_any, int_ref, load.at[1])
    amp_load.start()
    int_load.start()
    occ = amp_ref.shape[0]
    slots = amp_ref.shape[1]
    half = slots // 2
    row = lax.axis_index("row")
    col = lax.axis_index("col")
    core = lax.rem(col, 2)
    other = 1 - core
    chip = col // 2
    y = chip // 2
    z = lax.rem(row, 4)
    xh, xl = lax.rem(chip, 2), row // 4
    x = xh * 2 + xl

    def place_of(c, core_at):
        return spot(c // 16, c // 4 % 4, c % 4, core_at)

    def spot(x_at, y_at, z_at, core_at):
        return {"row": lax.rem(x_at, 2) * 4 + z_at, "col": (y_at * 2 + x_at // 2) * 2 + core_at}

    x1 = x + 1 - 2 * lax.rem(x, 2)
    x2 = lax.rem(x + 2, 4)

    def mirror_of(c):
        xa, ya, za = c // 16, c // 4 % 4, c % 4
        return (za % 2 * 2 + ya // 2) * 16 + (xa % 2 * 2 + za // 2) * 4 + ya % 2 * 2 + xa // 2

    def look(table, at):
        value = jnp.int32(table[0])
        for n in range(1, len(table)):
            value = jnp.where(at == n, table[n], value)
        return value

    def inverse(table):
        turned = [0] * len(table)
        for n, v in enumerate(table):
            turned[v] = n
        return turned

    here = x * 16 + y * 4 + z
    goes = [look(table, here) for table in RELAYS]
    comes = [look(inverse(table), here) for table in RELAYS]
    ends = [mirror_of(c) for c in comes]
    hands = [look(table, mirror_of(here)) for table in RELAYS]

    barrier = pltpu.get_barrier_semaphore()

    def greet(place):
        pl.semaphore_signal(barrier, inc=1, device_id=place, device_id_type=MESH)

    greet(spot(x, y, z, other))
    for step in range(1, 4):
        for e in range(2):
            greet(spot(lax.rem(x + step, 4), y, z, e))
            greet(spot(x, y, lax.rem(z + step, 4), e))
    for step in range(1, 4):
        for e in range(2):
            greet(spot(x, lax.rem(y + step, 4), z, e))
            greet(spot(x1, y, lax.rem(z + step, 4), e))

    total = jnp.int32(25)
    for n in range(len(RELAYS)):
        @pl.when(comes[n] != here)
        def _(n=n):
            greet(place_of(comes[n], core))

        @pl.when(hands[n] != here)
        def _(n=n):
            for e in range(2):
                greet(place_of(hands[n], e))

        total = total + jnp.where(goes[n] != here, 1, 0) + jnp.where(ends[n] != here, 2, 0)


    def remote(src, dst, send, recv, place):
        return pltpu.make_async_remote_copy(
            src_ref=src, dst_ref=dst, send_sem=send, recv_sem=recv, device_id=place, device_id_type=MESH
        )

    def arrived(buf, sem):
        pltpu.make_async_copy(buf, buf, sem).wait()

    def choose(cond, yes, no):
        pl.when(cond)(yes)
        pl.when(jnp.logical_not(cond))(no)

    def pack_a():
        for i in range(occ):
            wide[...] = amp_ref[i].reshape(slots * TILE, LANES).astype(jnp.float32)
            left = wide[pl.ds(0, slots * HALF, stride=2), :].astype(jnp.bfloat16)
            right = wide[pl.ds(1, slots * HALF, stride=2), :].astype(jnp.bfloat16)
            both = jnp.concatenate([left, right], axis=1)
            made = jnp.dot(both, amat_ref[...], preferred_element_type=jnp.float32).astype(jnp.bfloat16)
            for s in range(slots):
                for h in range(2):
                    a_out[s % half // span, s // half, s % span, pl.ds(i * TILE + h * HALF, HALF), :] = made[
                        s * HALF : (s + 1) * HALF, h * LANES : (h + 1) * LANES
                    ]

    def pack_w(p):
        @pl.loop(0, 8)
        def _(r):
            xi, zd = r // 4, lax.rem(r, 4)
            for e in range(2):
                for u in range(span):
                    tile = list_ref[r, 1, e * half + p * span + u]
                    at = (e * span + u) * occ * TILE
                    wide[pl.ds(at, occ * TILE), :] = int_ref[:, tile].reshape(occ * TILE, LANES).astype(jnp.float32)
                    left = wide[pl.ds(at, occ * HALF, stride=2), :].astype(jnp.bfloat16)
                    right = wide[pl.ds(at + 1, occ * HALF, stride=2), :].astype(jnp.bfloat16)
                    both = jnp.concatenate([left, right], axis=1)
                    made = jnp.dot(both, wmat_ref[...], preferred_element_type=jnp.float32).astype(jnp.bfloat16)
                    for k in range(occ):
                        for g in range(2):
                            w_out[p, zd, e, u, xi, pl.ds(k * TILE + g * HALF, HALF), :] = made[
                                k * HALF : (k + 1) * HALF, g * LANES : (g + 1) * LANES
                            ]

    def y_copies(p):
        n = p
        here = abuf.at[p, xh, y, core]
        copies = []
        for e in range(2):
            copies.append(remote(a_out.at[p, e], here, y_send.at[n, 4, e], y_recv.at[n, xh, y, core], spot(x2, y, z, e)))
        for step in (1, 3, 2):
            for e in range(2):
                place = spot(x, lax.rem(y + step, 4), z, e)
                copies.append(remote(a_out.at[p, e], here, y_send.at[n, step, e], y_recv.at[n, xh, y, core], place))
        copies.append(remote(a_out.at[p, other], here, y_send.at[n, 0, 0], y_recv.at[n, xh, y, core], spot(x, y, z, other)))
        return copies

    def send_y(p):
        for copy in y_copies(p):
            copy.start()
        n = p
        pltpu.make_async_copy(a_out.at[p, core], abuf.at[p, xh, y, core], y_recv.at[n, xh, y, core]).start()

    def pass_copies(p):
        n = p
        copies = []
        for step in (1, 3, 2):
            for e in range(2):
                block = abuf.at[p, 1 - xh, y, e]
                place = spot(x, lax.rem(y + step, 4), z, core)
                copies.append(remote(block, block, x_send.at[n, step, e], y_recv.at[n, 1 - xh, y, e], place))
        return copies

    def pass_on(p):
        n = p
        for e in range(2):
            arrived(abuf.at[p, 1 - xh, y, e], y_recv.at[n, 1 - xh, y, e])
        for copy in pass_copies(p):
            copy.start()

    def v_copies(p):
        n = p
        copies = []
        for flip in (1, 0):
            for step in (1, 3, 2, 0):
                zd = lax.rem(z + step, 4)
                to = lax.rem(xl + flip, 2)
                for e in range(2):
                    if flip or step:
                        place = spot(xh * 2 + to, y, zd, e)
                        copies.append(
                            remote(
                                w_out.at[p, zd, e, :, to], wbuf.at[p, z, core, :, xl],
                                v_send.at[n, flip, step, e], v_recv.at[n, z, core, xl], place,
                            )
                        )
        copies.append(
            remote(
                w_out.at[p, z, other, :, xl], wbuf.at[p, z, core, :, xl],
                v_send.at[n, 0, 0, 0], v_recv.at[n, z, core, xl], spot(x, y, z, other),
            )
        )
        return copies

    def send_v(p):
        for copy in v_copies(p):
            copy.start()
        n = p
        pltpu.make_async_copy(
            w_out.at[p, z, core, :, xl], wbuf.at[p, z, core, :, xl], v_recv.at[n, z, core, xl]
        ).start()

    def compute(p):
        n = p
        for a in range(2):
            for b in range(4):
                for e in range(2):

                    @pl.when(jnp.logical_or(a == xh, b != y))
                    def _(a=a, b=b, e=e):
                        arrived(abuf.at[p, a, b, e], y_recv.at[n, a, b, e])

        for zs in range(4):
            for e in range(2):
                for ks in range(2):
                    arrived(wbuf.at[p, zs, e, :, ks], v_recv.at[n, zs, e, ks])

        @pl.loop(0, span)
        def _(u):
            total = jnp.zeros((4 * TILE, 4 * TILE), jnp.float32)
            for zs in range(4):
                for ks in range(2):
                    b = ks * 2 + zs // 2
                    left = jnp.concatenate([abuf[p, zs % 2, b, 0, u], abuf[p, zs % 2, b, 1, u]], axis=1)
                    right = jnp.concatenate([wbuf[p, zs, 0, u, ks], wbuf[p, zs, 1, u, ks]], axis=1)
                    total = total + jnp.dot(left, right, preferred_element_type=jnp.float32)
            keep_sum(p, u, total)

        emit(p)

    def p_copy(p):
        return remote(cbuf.at[p, :, other], own_ref.at[core, p], p_send.at[p], p_recv.at[p], spot(x, y, z, other))

    def k_copy(p):
        return pltpu.make_async_copy(cbuf.at[p, :, core], own_ref.at[core, p], keep.at[p])

    def m_copy(p):
        return remote(cbuf.at[p], mbuf.at[p], m_send.at[p], m_recv.at[p], place_of(goes[p % len(RELAYS)], core))

    def n_copy(p, q, place):
        return remote(mbuf.at[p, q], mir_ref.at[core, p], n_send.at[p, q], n_recv.at[p, core], place)

    def keep_sum(p, u, total):
        made = total.astype(jnp.bfloat16)
        for q in range(2):
            for j in range(2):
                cbuf[p, q, j, u] = made[q * LANES : (q + 1) * LANES, j * LANES : (j + 1) * LANES]

    def emit(p):
        def stay():
            pltpu.make_async_copy(cbuf.at[p], mbuf.at[p], m_recv.at[p]).start()

        choose(goes[p % len(RELAYS)] != here, lambda: m_copy(p).start(), stay)
        p_copy(p).start()
        k_copy(p).start()

    def relay(p):
        arrived(mbuf.at[p], m_recv.at[p])

        def away():
            for q in range(2):
                n_copy(p, q, place_of(ends[p % len(RELAYS)], q)).start()

        def within():
            n_copy(p, other, spot(x, y, z, other)).start()
            pltpu.make_async_copy(mbuf.at[p, core], mir_ref.at[core, p], n_recv.at[p, core]).start()

        choose(ends[p % len(RELAYS)] != here, away, within)

    def close(p):
        for e in range(2):
            arrived(mir_ref.at[e, p], n_recv.at[p, e])
        arrived(own_ref.at[other, p], p_recv.at[p])
        k_copy(p).wait()
        p_copy(p).wait_send()
        pl.when(goes[p % len(RELAYS)] != here)(lambda: m_copy(p).wait_send())

        def away():
            for q in range(2):
                arrived(mbuf.at[p, q], n_send.at[p, q])

        def within():
            arrived(mbuf.at[p, other], n_send.at[p, other])

        choose(ends[p % len(RELAYS)] != here, away, within)
        for copy in y_copies(p) + pass_copies(p) + v_copies(p):
            copy.wait_send()

    def find():
        for s in range(slots):
            a = list_ref[row, 0, s]
            b = list_ref[row, 1, s]
            found = jnp.int32(-1)
            for t in range(slots):
                same = (list_ref[chip, 0, t] == b) & (list_ref[chip, 1, t] == a)
                found = jnp.where(same & (t < count_ref[chip]), t, found)
            at_ref[0, s] = jnp.maximum(found, 0)
            at_ref[1, s] = (found >= 0).astype(jnp.int32)
            at_ref[2, s] = (s < count_ref[row]).astype(jnp.int32)

    amat_ref[...] = merge_matrix(True)
    wmat_ref[...] = merge_matrix(False)
    amp_load.wait()
    pack_a()
    int_load.wait()
    pack_w(0)
    pl.semaphore_wait(barrier, total)
    send_y(0)
    send_v(0)
    for p in range(1, min(A_AHEAD, phases)):
        send_y(p)
    for p in range(min(W_AHEAD, phases)):
        if p > 0:
            pack_w(p)
            send_v(p)
        if p == 0:
            pass_on(0)
    find()
    for p in range(phases):
        if p + A_AHEAD < phases:
            send_y(p + A_AHEAD)
        if p + 1 < phases:
            pass_on(p + 1)
        if p + W_AHEAD < phases:
            pack_w(p + W_AHEAD)
            send_v(p + W_AHEAD)
        compute(p)
        if p >= LAG:
            relay(p - LAG)
    for p in range(max(phases - LAG, 0), phases):
        relay(p)
    for p in range(phases):
        close(p)


def finish(at_ref, own_ref, mir_ref, mat_ref, out_ref, turn):
    slots = out_ref.shape[1]
    half = slots // 2
    span = own_ref.shape[3]
    lane = lax.broadcasted_iota(jnp.int32, (HALF, LANES), 1)
    low = lane < TILE

    def fold(even, odd):
        first = jnp.where(low, even, pltpu.roll(odd, TILE, 1))
        second = jnp.where(low, pltpu.roll(even, TILE, 1), odd)
        return first, second

    for s in range(slots):
        t = at_ref[0, s]
        hit = at_ref[1, s].astype(jnp.float32)
        live = at_ref[2, s].astype(jnp.float32)
        te, tp, tu = t // half, lax.rem(t, half) // span, lax.rem(t, span)
        se, sp, su = s // half, s % half // span, s % span
        for jp in range(2):
            block = mir_ref[te, tp, jp, tu]
            turned = lax.dot_general(block, mat_ref[...], (((0,), (0,)), ((), ())), preferred_element_type=jnp.float32)
            turn[s % 2, jp] = turned * hit
            mine = own_ref[se, sp, jp, su].astype(jnp.float32)
            for u in range(2):
                i = jp * 2 + u
                even = turn[s % 2, jp, pl.ds(u * TILE, HALF, stride=2), :]
                odd = turn[s % 2, jp, pl.ds(u * TILE + 1, HALF, stride=2), :]
                top = mine[u * TILE : u * TILE + HALF]
                bottom = mine[u * TILE + HALF : (u + 1) * TILE]
                first, second = fold((top + even) * live, (bottom + odd) * live)
                out_ref[i, s, pl.ds(0, HALF, stride=2), :] = first
                out_ref[i, s, pl.ds(1, HALF, stride=2), :] = second


def on_device(amplitudes, integrals, pair_lists, tile_counts):
    occ_row, occ_col, slots, square = amplitudes.shape
    half = slots // 2
    span = half // PHASES
    tiles = integrals.shape[2]
    bf16 = jnp.bfloat16
    f32 = jnp.float32
    block = occ_row * TILE
    vmem = pl.BlockSpec(memory_space=pltpu.VMEM)
    smem = pl.BlockSpec(memory_space=pltpu.SMEM)
    anywhere = pl.BlockSpec(memory_space=pl.ANY)
    hbm = pl.BlockSpec(memory_space=pltpu.MemorySpace.HBM)
    dma = pltpu.SemaphoreType.DMA

    lists = pair_lists.transpose(0, 2, 1)
    amp = amplitudes.reshape(occ_row, occ_col, slots, HALF, LANES).transpose(0, 2, 3, 1, 4)
    amp = amp.reshape(occ_row, slots, TILE, LANES)
    integ = integrals.reshape(occ_row, occ_col, tiles, HALF, LANES).transpose(0, 2, 3, 1, 4)
    integ = integ.reshape(occ_row, tiles, TILE, LANES)

    own, mirror, places = pl.pallas_call(
        exchange,
        name="exchange",
        out_shape=(
            jax.ShapeDtypeStruct((2, PHASES, 2, span, LANES, LANES), bf16),
            jax.ShapeDtypeStruct((2, PHASES, 2, span, LANES, LANES), bf16),
            jax.ShapeDtypeStruct((3, slots), jnp.int32),
        ),
        in_specs=[smem, smem, hbm, hbm],
        out_specs=(anywhere, anywhere, smem),
        scratch_shapes=[
            pltpu.VMEM((occ_row, slots, TILE, LANES), bf16),
            pltpu.VMEM((occ_row, tiles, TILE, LANES), bf16),
            pltpu.VMEM((2 * LANES, 2 * LANES), bf16),
            pltpu.VMEM((2 * LANES, 2 * LANES), bf16),
            pltpu.VMEM((PHASES, 2, span, block, LANES), bf16),
            pltpu.VMEM((PHASES, 4, 2, span, 2, block, LANES), bf16),
            pltpu.VMEM((PHASES, 2, 4, 2, span, block, LANES), bf16),
            pltpu.VMEM((PHASES, 4, 2, span, 2, block, LANES), bf16),
            pltpu.VMEM((PHASES, 2, 2, span, LANES, LANES), bf16),
            pltpu.VMEM((PHASES, 2, 2, span, LANES, LANES), bf16),
            pltpu.VMEM((max(slots * TILE, 2 * span * block), LANES), f32),
            dma((2,)),
            dma((PHASES, 5, 2)),
            dma((PHASES, 2, 4, 2)),
            dma((PHASES, 4, 2)),
            dma((PHASES, 2, 4, 2)),
            dma((PHASES, 4, 2, 2)),
            dma((PHASES,)),
            dma((PHASES,)),
            dma((PHASES,)),
            dma((PHASES,)),
            dma((PHASES,)),
            dma((PHASES, 2)),
            dma((PHASES, 2)),
        ],
        compiler_params=pltpu.CompilerParams(collective_id=0, has_side_effects=True, vmem_limit_bytes=62 << 20),
    )(lists, tile_counts, amp, integ)

    packed = pl.pallas_call(
        finish,
        name="finish",
        out_shape=jax.ShapeDtypeStruct((occ_row, slots, TILE, LANES), f32),
        in_specs=[smem, vmem, vmem, vmem],
        out_specs=vmem,
        scratch_shapes=[pltpu.VMEM((2, 2, LANES, LANES), f32)],
        compiler_params=pltpu.CompilerParams(vmem_limit_bytes=32 << 20),
    )(places, own, mirror, jnp.asarray(untangle_matrix(), bf16))
    packed = packed.reshape(occ_row, slots, HALF, occ_col, LANES).transpose(0, 3, 1, 2, 4)
    return packed.reshape(occ_row, occ_col, slots, square)


def solution(mesh):
    return jax.shard_map(
        on_device,
        mesh=mesh,
        in_specs=(P("row", "col", None, None), P("row", "col", None, None), P(), P()),
        out_specs=P("row", "col", None, None),
        check_vma=False,
    )
```

```python
import functools

import jax
import jax.numpy as jnp
from jax import lax
from jax.experimental import pallas as pl
from jax.experimental.pallas import tpu as pltpu
from jax.sharding import PartitionSpec as P

MESH = pl.DeviceIdType.MESH
ROWS = 8
TILE = 64
HALF = TILE // 2
LANES = 128
PHASES = 6
A_AHEAD = 2
W_AHEAD = 2
LAG = 2
RELAYS = (
    (63, 48, 55, 56, 51, 54, 2, 7, 8, 0, 35, 52, 49, 50, 4, 10, 43, 33, 44, 41, 26, 45, 31, 18, 21, 24, 16, 40, 29, 42, 20, 46, 17, 32, 30, 39, 19, 27, 6, 28, 34, 36, 25, 38, 23, 47, 37, 5, 62, 60, 53, 61, 9, 14, 3, 15, 57, 58, 1, 13, 22, 11, 12, 59),
    (12, 5, 41, 55, 54, 50, 7, 10, 3, 58, 52, 60, 2, 62, 39, 48, 28, 40, 21, 47, 42, 22, 37, 46, 24, 44, 31, 19, 26, 34, 43, 30, 29, 45, 36, 25, 20, 16, 27, 38, 32, 6, 33, 17, 18, 1, 23, 35, 4, 57, 0, 14, 8, 51, 61, 63, 56, 53, 13, 9, 11, 59, 15, 49),
    (48, 0, 56, 36, 14, 3, 10, 2, 61, 51, 5, 4, 54, 55, 6, 50, 24, 42, 47, 44, 25, 26, 34, 40, 31, 29, 28, 32, 30, 22, 46, 45, 16, 17, 1, 20, 18, 35, 23, 37, 21, 33, 38, 41, 19, 43, 27, 39, 11, 53, 13, 49, 7, 52, 8, 59, 9, 57, 62, 12, 60, 63, 58, 15),
)


def merge_matrix(permute):
    row = lax.broadcasted_iota(jnp.int32, (2 * LANES, 2 * LANES), 0)
    col = lax.broadcasted_iota(jnp.int32, (2 * LANES, 2 * LANES), 1)
    c = row & (TILE - 1)
    place = (c & 1) * HALF + (c >> 1) if permute else c
    target = ((row >> 6) & 1) * LANES + (row >> 7) * TILE + place
    return jnp.where(col == target, 1.0, 0.0).astype(jnp.bfloat16)


def untangle_matrix():
    row = lax.broadcasted_iota(jnp.int32, (LANES, LANES), 0)
    col = lax.broadcasted_iota(jnp.int32, (LANES, LANES), 1)
    target = (row & TILE) + (row & (HALF - 1)) * 2 + ((row >> 5) & 1)
    return jnp.where(col == target, 1.0, 0.0).astype(jnp.bfloat16)


def exchange(
    list_ref, count_ref, amp_any, int_any, own_ref, mir_ref, at_ref,
    amp_ref, int_ref, amat_ref, wmat_ref, a_out, w_out, abuf, wbuf, cbuf, mbuf, wide, load,
    y_send, y_recv, x_send, v_send, v_recv, p_send, p_recv, keep, m_send, m_recv, n_send, n_recv,
):
    phases, _, span = a_out.shape[:3]
    amp_load = pltpu.make_async_copy(amp_any, amp_ref, load.at[0])
    int_load = pltpu.make_async_copy(int_any, int_ref, load.at[1])
    amp_load.start()
    int_load.start()
    occ = amp_ref.shape[0]
    slots = amp_ref.shape[1]
    half = slots // 2
    row = lax.axis_index("row")
    col = lax.axis_index("col")
    core = lax.rem(col, 2)
    other = 1 - core
    chip = col // 2
    y = chip // 2
    z = lax.rem(row, 4)
    xh, xl = lax.rem(chip, 2), row // 4
    x = xh * 2 + xl

    def place_of(c, core_at):
        return spot(c // 16, c // 4 % 4, c % 4, core_at)

    def spot(x_at, y_at, z_at, core_at):
        return {"row": lax.rem(x_at, 2) * 4 + z_at, "col": (y_at * 2 + x_at // 2) * 2 + core_at}

    x1 = x + 1 - 2 * lax.rem(x, 2)
    x2 = lax.rem(x + 2, 4)

    def mirror_of(c):
        xa, ya, za = c // 16, c // 4 % 4, c % 4
        return (za % 2 * 2 + ya // 2) * 16 + (xa % 2 * 2 + za // 2) * 4 + ya % 2 * 2 + xa // 2

    def look(table, at):
        value = jnp.int32(table[0])
        for n in range(1, len(table)):
            value = jnp.where(at == n, table[n], value)
        return value

    def inverse(table):
        turned = [0] * len(table)
        for n, v in enumerate(table):
            turned[v] = n
        return turned

    here = x * 16 + y * 4 + z
    goes = [look(table, here) for table in RELAYS]
    comes = [look(inverse(table), here) for table in RELAYS]
    ends = [mirror_of(c) for c in comes]
    hands = [look(table, mirror_of(here)) for table in RELAYS]

    barrier = pltpu.get_barrier_semaphore()

    def greet(place):
        pl.semaphore_signal(barrier, inc=1, device_id=place, device_id_type=MESH)

    greet(spot(x, y, z, other))
    for step in range(1, 4):
        for e in range(2):
            greet(spot(lax.rem(x + step, 4), y, z, e))
            greet(spot(x, y, lax.rem(z + step, 4), e))
    for step in range(1, 4):
        for e in range(2):
            greet(spot(x, lax.rem(y + step, 4), z, e))
            greet(spot(x1, y, lax.rem(z + step, 4), e))

    total = jnp.int32(25)
    for n in range(len(RELAYS)):
        @pl.when(comes[n] != here)
        def _(n=n):
            greet(place_of(comes[n], core))

        @pl.when(hands[n] != here)
        def _(n=n):
            for e in range(2):
                greet(place_of(hands[n], e))

        total = total + jnp.where(goes[n] != here, 1, 0) + jnp.where(ends[n] != here, 2, 0)


    def remote(src, dst, send, recv, place):
        return pltpu.make_async_remote_copy(
            src_ref=src, dst_ref=dst, send_sem=send, recv_sem=recv, device_id=place, device_id_type=MESH
        )

    def arrived(buf, sem):
        pltpu.make_async_copy(buf, buf, sem).wait()

    def choose(cond, yes, no):
        pl.when(cond)(yes)
        pl.when(jnp.logical_not(cond))(no)

    def pack_a():
        for i in range(occ):
            wide[...] = amp_ref[i].reshape(slots * TILE, LANES).astype(jnp.float32)
            left = wide[pl.ds(0, slots * HALF, stride=2), :].astype(jnp.bfloat16)
            right = wide[pl.ds(1, slots * HALF, stride=2), :].astype(jnp.bfloat16)
            both = jnp.concatenate([left, right], axis=1)
            made = jnp.dot(both, amat_ref[...], preferred_element_type=jnp.float32).astype(jnp.bfloat16)
            for s in range(slots):
                for h in range(2):
                    a_out[s % half // span, s // half, s % span, pl.ds(i * TILE + h * HALF, HALF), :] = made[
                        s * HALF : (s + 1) * HALF, h * LANES : (h + 1) * LANES
                    ]

    def pack_w(p):
        @pl.loop(0, 8)
        def _(r):
            xi, zd = r // 4, lax.rem(r, 4)
            for e in range(2):
                for u in range(span):
                    tile = list_ref[r, 1, e * half + p * span + u]
                    at = (e * span + u) * occ * TILE
                    wide[pl.ds(at, occ * TILE), :] = int_ref[:, tile].reshape(occ * TILE, LANES).astype(jnp.float32)
                    left = wide[pl.ds(at, occ * HALF, stride=2), :].astype(jnp.bfloat16)
                    right = wide[pl.ds(at + 1, occ * HALF, stride=2), :].astype(jnp.bfloat16)
                    both = jnp.concatenate([left, right], axis=1)
                    made = jnp.dot(both, wmat_ref[...], preferred_element_type=jnp.float32).astype(jnp.bfloat16)
                    for k in range(occ):
                        for g in range(2):
                            w_out[p, zd, e, u, xi, pl.ds(k * TILE + g * HALF, HALF), :] = made[
                                k * HALF : (k + 1) * HALF, g * LANES : (g + 1) * LANES
                            ]

    def y_copies(p):
        n = p
        here = abuf.at[p, xh, y, core]
        copies = []
        for e in range(2):
            copies.append(remote(a_out.at[p, e], here, y_send.at[n, 4, e], y_recv.at[n, xh, y, core], spot(x2, y, z, e)))
        for step in (1, 3, 2):
            for e in range(2):
                place = spot(x, lax.rem(y + step, 4), z, e)
                copies.append(remote(a_out.at[p, e], here, y_send.at[n, step, e], y_recv.at[n, xh, y, core], place))
        copies.append(remote(a_out.at[p, other], here, y_send.at[n, 0, 0], y_recv.at[n, xh, y, core], spot(x, y, z, other)))
        return copies

    def send_y(p):
        for copy in y_copies(p):
            copy.start()
        n = p
        pltpu.make_async_copy(a_out.at[p, core], abuf.at[p, xh, y, core], y_recv.at[n, xh, y, core]).start()

    def pass_copies(p):
        n = p
        copies = []
        for step in (1, 3, 2):
            for e in range(2):
                block = abuf.at[p, 1 - xh, y, e]
                place = spot(x, lax.rem(y + step, 4), z, core)
                copies.append(remote(block, block, x_send.at[n, step, e], y_recv.at[n, 1 - xh, y, e], place))
        return copies

    def pass_on(p):
        n = p
        for e in range(2):
            arrived(abuf.at[p, 1 - xh, y, e], y_recv.at[n, 1 - xh, y, e])
        for copy in pass_copies(p):
            copy.start()

    def v_copies(p):
        n = p
        copies = []
        for flip in (1, 0):
            for step in (1, 3, 2, 0):
                zd = lax.rem(z + step, 4)
                to = lax.rem(xl + flip, 2)
                for e in range(2):
                    if flip or step:
                        place = spot(xh * 2 + to, y, zd, e)
                        copies.append(
                            remote(
                                w_out.at[p, zd, e, :, to], wbuf.at[p, z, core, :, xl],
                                v_send.at[n, flip, step, e], v_recv.at[n, z, core, xl], place,
                            )
                        )
        copies.append(
            remote(
                w_out.at[p, z, other, :, xl], wbuf.at[p, z, core, :, xl],
                v_send.at[n, 0, 0, 0], v_recv.at[n, z, core, xl], spot(x, y, z, other),
            )
        )
        return copies

    def send_v(p):
        for copy in v_copies(p):
            copy.start()
        n = p
        pltpu.make_async_copy(
            w_out.at[p, z, core, :, xl], wbuf.at[p, z, core, :, xl], v_recv.at[n, z, core, xl]
        ).start()

    def compute(p):
        n = p
        for a in range(2):
            for b in range(4):
                for e in range(2):

                    @pl.when(jnp.logical_or(a == xh, b != y))
                    def _(a=a, b=b, e=e):
                        arrived(abuf.at[p, a, b, e], y_recv.at[n, a, b, e])

        for zs in range(4):
            for e in range(2):
                for ks in range(2):
                    arrived(wbuf.at[p, zs, e, :, ks], v_recv.at[n, zs, e, ks])

        @pl.loop(0, span)
        def _(u):
            total = jnp.zeros((4 * TILE, 4 * TILE), jnp.float32)
            for zs in range(4):
                for ks in range(2):
                    b = ks * 2 + zs // 2
                    left = jnp.concatenate([abuf[p, zs % 2, b, 0, u], abuf[p, zs % 2, b, 1, u]], axis=1)
                    right = jnp.concatenate([wbuf[p, zs, 0, u, ks], wbuf[p, zs, 1, u, ks]], axis=1)
                    total = total + jnp.dot(left, right, preferred_element_type=jnp.float32)
            keep_sum(p, u, total)

        emit(p)

    def p_copy(p):
        return remote(cbuf.at[p, :, other], own_ref.at[core, p], p_send.at[p], p_recv.at[p], spot(x, y, z, other))

    def k_copy(p):
        return pltpu.make_async_copy(cbuf.at[p, :, core], own_ref.at[core, p], keep.at[p])

    def m_copy(p):
        return remote(cbuf.at[p], mbuf.at[p], m_send.at[p], m_recv.at[p], place_of(goes[p % len(RELAYS)], core))

    def n_copy(p, q, place):
        return remote(mbuf.at[p, q], mir_ref.at[core, p], n_send.at[p, q], n_recv.at[p, core], place)

    def keep_sum(p, u, total):
        made = total.astype(jnp.bfloat16)
        for q in range(2):
            for j in range(2):
                cbuf[p, q, j, u] = made[q * LANES : (q + 1) * LANES, j * LANES : (j + 1) * LANES]

    def emit(p):
        def stay():
            pltpu.make_async_copy(cbuf.at[p], mbuf.at[p], m_recv.at[p]).start()

        choose(goes[p % len(RELAYS)] != here, lambda: m_copy(p).start(), stay)
        p_copy(p).start()
        k_copy(p).start()

    def relay(p):
        arrived(mbuf.at[p], m_recv.at[p])

        def away():
            for q in range(2):
                n_copy(p, q, place_of(ends[p % len(RELAYS)], q)).start()

        def within():
            n_copy(p, other, spot(x, y, z, other)).start()
            pltpu.make_async_copy(mbuf.at[p, core], mir_ref.at[core, p], n_recv.at[p, core]).start()

        choose(ends[p % len(RELAYS)] != here, away, within)

    def close(p):
        for e in range(2):
            arrived(mir_ref.at[e, p], n_recv.at[p, e])
        arrived(own_ref.at[other, p], p_recv.at[p])
        k_copy(p).wait()
        p_copy(p).wait_send()
        pl.when(goes[p % len(RELAYS)] != here)(lambda: m_copy(p).wait_send())

        def away():
            for q in range(2):
                arrived(mbuf.at[p, q], n_send.at[p, q])

        def within():
            arrived(mbuf.at[p, other], n_send.at[p, other])

        choose(ends[p % len(RELAYS)] != here, away, within)
        for copy in y_copies(p) + pass_copies(p) + v_copies(p):
            copy.wait_send()

    def find():
        for s in range(slots):
            a = list_ref[row, 0, s]
            b = list_ref[row, 1, s]
            found = jnp.int32(-1)
            for t in range(slots):
                same = (list_ref[chip, 0, t] == b) & (list_ref[chip, 1, t] == a)
                found = jnp.where(same & (t < count_ref[chip]), t, found)
            at_ref[0, s] = jnp.maximum(found, 0)
            at_ref[1, s] = (found >= 0).astype(jnp.int32)
            at_ref[2, s] = (s < count_ref[row]).astype(jnp.int32)

    amat_ref[...] = merge_matrix(True)
    wmat_ref[...] = merge_matrix(False)
    amp_load.wait()
    pack_a()
    int_load.wait()
    pack_w(0)
    pl.semaphore_wait(barrier, total)
    send_y(0)
    send_v(0)
    for p in range(1, min(A_AHEAD, phases)):
        send_y(p)
    for p in range(min(W_AHEAD, phases)):
        if p > 0:
            pack_w(p)
            send_v(p)
        if p == 0:
            pass_on(0)
    find()
    for p in range(phases):
        if p + A_AHEAD < phases:
            send_y(p + A_AHEAD)
        if p + 1 < phases:
            pass_on(p + 1)
        if p + W_AHEAD < phases:
            pack_w(p + W_AHEAD)
            send_v(p + W_AHEAD)
        compute(p)
        if p >= LAG:
            relay(p - LAG)
    for p in range(max(phases - LAG, 0), phases):
        relay(p)
    for p in range(phases):
        close(p)


def finish(at_ref, own_any, mir_any, out_ref, own_ref, mir_ref, turn, load):
    copies = [pltpu.make_async_copy(own_any, own_ref, load.at[0]), pltpu.make_async_copy(mir_any, mir_ref, load.at[1])]
    for copy in copies:
        copy.start()
    matrix = untangle_matrix()
    slots = out_ref.shape[1]
    half = slots // 2
    span = own_ref.shape[3]
    lane = lax.broadcasted_iota(jnp.int32, (HALF, LANES), 1)
    low = lane < TILE

    def fold(even, odd):
        first = jnp.where(low, even, pltpu.roll(odd, TILE, 1))
        second = jnp.where(low, pltpu.roll(even, TILE, 1), odd)
        return first, second

    for copy in copies:
        copy.wait()
    for s in range(slots):
        t = at_ref[0, s]
        hit = at_ref[1, s].astype(jnp.float32)
        live = at_ref[2, s].astype(jnp.float32)
        te, tp, tu = t // half, lax.rem(t, half) // span, lax.rem(t, span)
        se, sp, su = s // half, s % half // span, s % span
        for jp in range(2):
            block = mir_ref[te, tp, jp, tu]
            turned = lax.dot_general(block, matrix, (((0,), (0,)), ((), ())), preferred_element_type=jnp.float32)
            turn[s % 2, jp] = turned * hit
            mine = own_ref[se, sp, jp, su].astype(jnp.float32)
            for u in range(2):
                i = jp * 2 + u
                even = turn[s % 2, jp, pl.ds(u * TILE, HALF, stride=2), :]
                odd = turn[s % 2, jp, pl.ds(u * TILE + 1, HALF, stride=2), :]
                top = mine[u * TILE : u * TILE + HALF]
                bottom = mine[u * TILE + HALF : (u + 1) * TILE]
                first, second = fold((top + even) * live, (bottom + odd) * live)
                out_ref[i, s, pl.ds(0, HALF, stride=2), :] = first
                out_ref[i, s, pl.ds(1, HALF, stride=2), :] = second


def on_device(amplitudes, integrals, pair_lists, tile_counts):
    occ_row, occ_col, slots, square = amplitudes.shape
    half = slots // 2
    span = half // PHASES
    tiles = integrals.shape[2]
    bf16 = jnp.bfloat16
    f32 = jnp.float32
    block = occ_row * TILE
    vmem = pl.BlockSpec(memory_space=pltpu.VMEM)
    smem = pl.BlockSpec(memory_space=pltpu.SMEM)
    anywhere = pl.BlockSpec(memory_space=pl.ANY)
    hbm = pl.BlockSpec(memory_space=pltpu.MemorySpace.HBM)
    dma = pltpu.SemaphoreType.DMA

    lists = pair_lists.transpose(0, 2, 1)
    amp = amplitudes.reshape(occ_row, occ_col, slots, HALF, LANES).transpose(0, 2, 3, 1, 4)
    amp = amp.reshape(occ_row, slots, TILE, LANES)
    integ = integrals.reshape(occ_row, occ_col, tiles, HALF, LANES).transpose(0, 2, 3, 1, 4)
    integ = integ.reshape(occ_row, tiles, TILE, LANES)

    own, mirror, places = pl.pallas_call(
        exchange,
        name="exchange",
        out_shape=(
            jax.ShapeDtypeStruct((2, PHASES, 2, span, LANES, LANES), bf16),
            jax.ShapeDtypeStruct((2, PHASES, 2, span, LANES, LANES), bf16),
            jax.ShapeDtypeStruct((3, slots), jnp.int32),
        ),
        in_specs=[smem, smem, hbm, hbm],
        out_specs=(anywhere, anywhere, smem),
        scratch_shapes=[
            pltpu.VMEM((occ_row, slots, TILE, LANES), bf16),
            pltpu.VMEM((occ_row, tiles, TILE, LANES), bf16),
            pltpu.VMEM((2 * LANES, 2 * LANES), bf16),
            pltpu.VMEM((2 * LANES, 2 * LANES), bf16),
            pltpu.VMEM((PHASES, 2, span, block, LANES), bf16),
            pltpu.VMEM((PHASES, 4, 2, span, 2, block, LANES), bf16),
            pltpu.VMEM((PHASES, 2, 4, 2, span, block, LANES), bf16),
            pltpu.VMEM((PHASES, 4, 2, span, 2, block, LANES), bf16),
            pltpu.VMEM((PHASES, 2, 2, span, LANES, LANES), bf16),
            pltpu.VMEM((PHASES, 2, 2, span, LANES, LANES), bf16),
            pltpu.VMEM((max(slots * TILE, 2 * span * block), LANES), f32),
            dma((2,)),
            dma((PHASES, 5, 2)),
            dma((PHASES, 2, 4, 2)),
            dma((PHASES, 4, 2)),
            dma((PHASES, 2, 4, 2)),
            dma((PHASES, 4, 2, 2)),
            dma((PHASES,)),
            dma((PHASES,)),
            dma((PHASES,)),
            dma((PHASES,)),
            dma((PHASES,)),
            dma((PHASES, 2)),
            dma((PHASES, 2)),
        ],
        compiler_params=pltpu.CompilerParams(collective_id=0, has_side_effects=True, vmem_limit_bytes=62 << 20),
    )(lists, tile_counts, amp, integ)

    packed = pl.pallas_call(
        finish,
        name="finish",
        out_shape=jax.ShapeDtypeStruct((occ_row, slots, TILE, LANES), f32),
        in_specs=[smem, hbm, hbm],
        out_specs=vmem,
        scratch_shapes=[
            pltpu.VMEM(own.shape, bf16),
            pltpu.VMEM(mirror.shape, bf16),
            pltpu.VMEM((2, 2, LANES, LANES), f32),
            dma((2,)),
        ],
        compiler_params=pltpu.CompilerParams(vmem_limit_bytes=62 << 20),
    )(places, own, mirror)
    packed = packed.reshape(occ_row, slots, HALF, occ_col, LANES).transpose(0, 3, 1, 2, 4)
    return packed.reshape(occ_row, occ_col, slots, square)


def solution(mesh):
    return jax.shard_map(
        on_device,
        mesh=mesh,
        in_specs=(P("row", "col", None, None), P("row", "col", None, None), P(), P()),
        out_specs=P("row", "col", None, None),
        check_vma=False,
    )
```
